512 devices in a mesh: seq: 128 (over x_hi, y, z), dp: 4 (over x_lo, core).
Axes of the slice: x: 4 (x_hi: 2, x_lo: 2; x = x_hi * 2 + x_lo), y: 4, z: 16, core: 2. Of those that a mesh axis runs over, the one named last changes fastest.
Arguments:
- asking_vectors: bfloat16 [4, 16384, 2048], P('dp', 'seq'), may hold values from -100 to 100
- lookup_vectors: bfloat16 [4, 16384, 2048], P('dp', 'seq'), may hold values from -13 to 13
- payload_vectors: bfloat16 [4, 16384, 2048], P('dp', 'seq'), may hold values from -6 to 6
- incoming_sensitivity: bfloat16 [4, 16384, 2048], P('dp', 'seq'), may hold values from -6 to 6
- learned_sharpness: float32 [16], replicated, may hold values from 0.5 to 2
- reply_list_sizes: int32 [4, 8], P('dp'), may hold values from 1 to 8192, 16384 in all within a row
Outputs:
- attention_result: bfloat16 [4, 16384, 2048], P('dp', 'seq')
- query_gradient: bfloat16 [4, 16384, 2048], P('dp', 'seq')
- key_gradient: bfloat16 [4, 16384, 2048], P('dp', 'seq')
- value_gradient: bfloat16 [4, 16384, 2048], P('dp', 'seq')
- scale_gradient: float32 [16], replicated
The draws below stay inside these ranges and needn't reach their ends.
All inputs are finite; a program needn't handle non-finite values.
Results may differ from the reference program's by a relative error of at most 0.02.
The reference program's roundings to bfloat16 on the way count: a program that leaves them out, or rounds other values in their place, can miss the bound.
Values may be sent and summed in bfloat16 or wider, within the bound.
No kernel may reach another device: no remote copies, remote signals or barrier semaphores. Data moves between devices by JAX's collectives and lax.ppermute only.
A program may use at most 64 MiB of HBM per device.

```python
import math
import jax
import jax.numpy as jnp
import numpy as np
from jax import lax

MIXER_CHANNELS = 16
CHANNEL_SPAN = 128
TOK_DEV = 128
NDOC = 8
SEQ = 16384
BATCH = 4
N_SEQ = 128


def key_field(key):
    base = jnp.clip(jax.random.normal(jax.random.fold_in(key, 11), (BATCH, SEQ, MIXER_CHANNELS * CHANNEL_SPAN), jnp.float32), -6.0, 6.0)
    return base


def draw_lookup_vectors(key, part):
    return key_field(key).astype(jnp.bfloat16)


def draw_asking_vectors(key, part):
    base = jnp.clip(jax.random.normal(jax.random.fold_in(key, 21), (BATCH, SEQ, MIXER_CHANNELS * CHANNEL_SPAN), jnp.float32), -6.0, 6.0)
    return base.astype(jnp.bfloat16)


def steps_of(rng, shape, shards, smallest, largest):
    level = 1.0
    for dim, blocks in shards:
        heights = jax.random.uniform(jax.random.fold_in(jax.random.fold_in(rng, 6), dim), (blocks,), jnp.float32, smallest / len(shards), largest / len(shards))
        level = level * jnp.repeat(jnp.exp(heights), shape[dim] // blocks).reshape((-1,) + (1,) * (len(shape) - 1 - dim))
    return level


def length_profile(count, total, bound, lean):
    portions = [(1 << 20) // math.isqrt(grade ** lean) + 1 for grade in range(2, count + 1)]
    rest, counts = total - bound - (count - 1), [1] * (count - 1)
    while rest > 0:
        movable = [i for i in range(count - 1) if counts[i] < bound]
        pool, left = sum([portions[i] for i in movable]), rest
        for i in movable:
            addition = min(bound - counts[i], max(1, left * portions[i] // pool), rest)
            counts[i] = counts[i] + addition
            rest = rest - addition
    return np.array([bound] + counts)


def ragged(stream_key, number_of, total, reach, skew):
    if number_of == 2:
        one = jax.random.randint(stream_key, (), max(1, total - reach), min(reach, total - 1) + 1)
        return jnp.stack([one, total - one])
    sizes = jnp.asarray(length_profile(number_of, total, reach, skew), jnp.int32)
    couples = (number_of - 1) // 2
    source_of, receiver = sizes[1:1 + 2 * couples:2], sizes[2:2 + 2 * couples:2]
    margin = jnp.minimum(source_of - 1, reach - receiver)
    moved = jax.random.randint(jax.random.fold_in(stream_key, 1), (couples,), 0, 1 << 20) % (margin + 1)
    sizes = sizes.at[1:1 + 2 * couples:2].set(source_of - moved).at[2:2 + 2 * couples:2].set(receiver + moved)
    return sizes[jax.random.permutation(jax.random.fold_in(stream_key, 2), number_of)]


def centred(rng, dims, width, most, split=(), held_as=jnp.bfloat16):
    entries = width * jax.random.normal(rng, dims, jnp.float32)
    if split:
        entries = entries * steps_of(rng, dims, split, -0.22, 0.18)
    return jnp.clip(entries, -most, most).astype(held_as)


def setup_inputs(seed: int = 0) -> dict:
    splits = jax.random.split(jax.random.key(seed), 7)
    asking_vectors = draw_asking_vectors(jax.random.fold_in(splits[6], 71), 0)
    lookup_vectors = draw_lookup_vectors(jax.random.fold_in(splits[6], 71), 0)
    payload_vectors = centred(splits[2], (BATCH, SEQ, MIXER_CHANNELS * CHANNEL_SPAN), 1.0, 6.0, ((0, 4), (1, 128)))
    incoming_sensitivity = centred(splits[3], (BATCH, SEQ, MIXER_CHANNELS * CHANNEL_SPAN), 1.0, 6.0, ((0, 4), (1, 128)))
    learned_sharpness = jnp.clip(jnp.exp(jax.random.uniform(splits[4], (MIXER_CHANNELS,), jnp.float32, math.log(0.5), math.log(2.0))), 0.5, 2.0)
    reply_list_sizes = jax.vmap(lambda own: ragged(own, NDOC, SEQ, SEQ // 2, 2))(jax.random.split(splits[5], BATCH)).reshape((BATCH, NDOC)).astype(jnp.int32)
    return dict(asking_vectors=asking_vectors, lookup_vectors=lookup_vectors, payload_vectors=payload_vectors, incoming_sensitivity=incoming_sensitivity, learned_sharpness=learned_sharpness, reply_list_sizes=reply_list_sizes)


def level_plan(level_idx, head_idx, seq_devices):
    group_span = min(2 ** level_idx, seq_devices)
    dilation = max(1, group_span // 4)
    offset = (5 + head_idx * (dilation // 2)) % dilation
    return (group_span, dilation, offset)

def doc_of(positions, lengths_row):
    doc_ends = jnp.cumsum(lengths_row)[:-1]
    return lax.optimization_barrier(jnp.sum((positions[:, None] >= doc_ends[None, :]).astype(jnp.int32), axis=1))

def reference(asking_vectors, lookup_vectors, payload_vectors, incoming_sensitivity, learned_sharpness, reply_list_sizes):
    positions = jnp.arange(SEQ, dtype=jnp.int32)
    outs_all, dq_all, dk_all, dv_all = ([], [], [], [])
    scale_terms = [jnp.zeros((), jnp.float32) for channel_count in range(MIXER_CHANNELS)]
    for batch_idx in range(BATCH):
        docs = doc_of(positions, reply_list_sizes[batch_idx])
        out_cols, dq_cols, dk_cols, dv_cols = ([], [], [], [])
        for level_idx in range(MIXER_CHANNELS // 2):
            for head_idx in range(2):
                group_span, dilation, offset = level_plan(level_idx, head_idx, N_SEQ)
                channel_count = 2 * level_idx + head_idx
                column = channel_count * CHANNEL_SPAN
                count = TOK_DEV * group_span // dilation
                segs = SEQ // (TOK_DEV * group_span)

                def picked_rows(source):
                    return source[batch_idx, offset::dilation, column:column + CHANNEL_SPAN].astype(jnp.float32).reshape(segs, count, CHANNEL_SPAN)
                qsel = picked_rows(asking_vectors)
                ksel = picked_rows(lookup_vectors)
                value_picked = picked_rows(payload_vectors)
                upstream_picked = picked_rows(incoming_sensitivity)
                doc_sel = docs[offset::dilation].reshape(segs, count)
                allowed = doc_sel[:, :, None] == doc_sel[:, None, :]
                raw = jnp.einsum('cte,cne->ctn', qsel, ksel, precision=lax.Precision.HIGHEST)
                logit_multiplier = learned_sharpness[channel_count] / math.sqrt(CHANNEL_SPAN)
                scores = jnp.where(allowed, raw * logit_multiplier, -jnp.inf)
                highest = lax.optimization_barrier(jnp.max(scores, axis=2, keepdims=True))
                expo = jnp.where(allowed, jnp.exp(scores - highest), 0.0)
                probs = expo / lax.optimization_barrier(jnp.sum(expo, axis=2, keepdims=True))
                probs_narrow = lax.optimization_barrier(probs.astype(jnp.bfloat16)).astype(jnp.float32)
                attended_output = jnp.einsum('lyj,ljc->lyc', probs_narrow, value_picked, precision=lax.Precision.HIGHEST)
                delta = lax.optimization_barrier(jnp.sum(upstream_picked * attended_output, axis=2, keepdims=True))
                gradient_probs = jnp.einsum('cte,cne->ctn', upstream_picked, value_picked, precision=lax.Precision.HIGHEST)
                dscores = probs * (gradient_probs - delta)
                scale_terms[channel_count] = scale_terms[channel_count] + jnp.sum(dscores * raw) / math.sqrt(CHANNEL_SPAN)
                ds_low = lax.optimization_barrier(dscores.astype(jnp.bfloat16)).astype(jnp.float32)
                grad_q = jnp.einsum('lyj,ljc->lyc', ds_low, ksel, precision=lax.Precision.HIGHEST) * logit_multiplier
                grad_k = jnp.einsum('sqk,sqd->skd', ds_low, qsel, precision=lax.Precision.HIGHEST) * logit_multiplier
                grad_v = jnp.einsum('sqk,sqd->skd', probs_narrow, upstream_picked, precision=lax.Precision.HIGHEST)

                def place(values_sel):
                    return jnp.zeros((SEQ, CHANNEL_SPAN), jnp.float32).at[offset::dilation].set(values_sel.reshape(-1, CHANNEL_SPAN))
                out_cols.append(place(attended_output))
                dq_cols.append(place(grad_q))
                dk_cols.append(place(grad_k))
                dv_cols.append(place(grad_v))
        outs_all.append(jnp.concatenate(out_cols, axis=1))
        dq_all.append(jnp.concatenate(dq_cols, axis=1))
        dk_all.append(jnp.concatenate(dk_cols, axis=1))
        dv_all.append(jnp.concatenate(dv_cols, axis=1))
    attention_result = jnp.stack(outs_all).astype(jnp.bfloat16)
    query_gradient = jnp.stack(dq_all).astype(jnp.bfloat16)
    key_gradient = jnp.stack(dk_all).astype(jnp.bfloat16)
    value_gradient = jnp.stack(dv_all).astype(jnp.bfloat16)
    scale_gradient = jnp.stack(scale_terms).astype(jnp.float32)
    return (attention_result, query_gradient, key_gradient, value_gradient, scale_gradient)
```

```python
import math

import jax
import jax.numpy as jnp
from jax import lax
from jax.experimental import pallas as pl
from jax.experimental.pallas import tpu as pltpu
from jax.sharding import Mesh, PartitionSpec as P

D = 128
BF = jnp.bfloat16
F32 = jnp.float32
DIL = (1, 1, 1, 2, 4, 8, 16, 32)
SEQ = ("x", "y", "q", "r")


def off(level, j):
    dil = DIL[level]
    return (5 + j * (dil // 2)) % dil


def iota(shape, dim):
    return lax.broadcasted_iota(jnp.int32, shape, dim)


def onehot(cond):
    return cond.astype(F32).astype(BF)


def mm(a, b):
    return jnp.dot(a, b, preferred_element_type=F32)


def mm_nt(a, b):
    return lax.dot_general(a, b, (((1,), (1,)), ((), ())), preferred_element_type=F32)


def mm_tn(a, b):
    return lax.dot_general(a, b, (((0,), (0,)), ((), ())), preferred_element_type=F32)


def pick(level, j, rows=128):
    n = 128 // DIL[level]
    return onehot(iota((n, 128), 1) == iota((n, 128), 0) * DIL[level] + off(level, j))


def cols(ref, head, first=0):
    return ref[:, pl.ds(pl.multiple_of((head - first) * D, D), D)]


def xyqr(dev):
    return dev >> 6, (dev >> 4) & 3, (dev >> 2) & 3, dev & 3


def xy_col(x, y, row):
    t, m = row >> 5, row & 31
    six = (x * 4 + (m >> 3)) * 32 + t * 8 + (m & 7)
    seven = (m >> 2) * 32 + t * 4 + (m & 3)
    return jnp.where(y < 2, six, jnp.where(y == 2, seven, -1))


def pack_kernel(ids, q_ref, k_ref, v_ref, u_ref, g1_ref, g3_ref, g5_ref, xy_ref):
    x, y, q, r = xyqr(ids[0])
    srcs = (q_ref, k_ref, v_ref, u_ref)
    h1 = 3 - (r & 1)
    j3 = 1 - (q & 1)
    j5 = 1 - (y & 1)
    s3, s5 = pick(3, j3), pick(5, j5)
    xy_ref[...] = jnp.zeros(xy_ref.shape, BF)
    for t, ref in enumerate(srcs):
        g1_ref[t * 128 : (t + 1) * 128] = cols(ref, h1)
        g3_ref[t * 64 : (t + 1) * 64] = mm(s3, cols(ref, 6 + j3)).astype(BF)
        g5_ref[t * 16 : (t + 1) * 16] = mm(s5, cols(ref, 10 + j5)).astype(BF)
    for j in range(2):
        acc6 = jnp.zeros((32, D), F32)
        acc7 = jnp.zeros((32, D), F32)
        ri, ci = iota((32, 128), 0), iota((32, 128), 1)
        for t, ref in enumerate(srcs):
            w6 = onehot((ci == (ri - t * 8) * 16 + off(6, j)))
            w7 = onehot((ci == (ri - t * 4) * 32 + off(7, j)))
            acc6 += mm(w6, ref[:, (12 + j) * D : (13 + j) * D])
            acc7 += mm(w7, ref[:, (14 + j) * D : (15 + j) * D])
        xy_ref[x * 4 + j] = acc6.astype(BF)
        xy_ref[j * 4 + 2] = acc7.astype(BF)


def to_q_kernel(ids, q_ref, k_ref, v_ref, u_ref, g5_ref, xy_ref, out_ref):
    x, y, q, r = xyqr(ids[0])
    j5 = y & 1
    s40, s41, s5 = pick(4, 0), pick(4, 1), pick(5, j5)
    for t, ref in enumerate((q_ref, k_ref, v_ref, u_ref)):
        out_ref[0, t * 32 : (t + 1) * 32] = mm(s40, ref[:, :D]).astype(BF)
        out_ref[1, t * 32 : (t + 1) * 32] = mm(s41, ref[:, D : 2 * D]).astype(BF)
        out_ref[2, t * 32 : t * 32 + 16] = mm(s5, cols(ref, 2 + j5)).astype(BF)
        out_ref[2, t * 32 + 16 : t * 32 + 32] = g5_ref[t * 16 : (t + 1) * 16]
    want = xy_col(x, y, iota((128, 256), 0))
    perm = onehot(want == iota((128, 256), 1))
    out_ref[3] = mm(perm, xy_ref[...].reshape(256, D)).astype(BF)


def to_r_kernel(ids, q_ref, k_ref, v_ref, u_ref, g3_ref, qr_ref, out_ref):
    x, y, q, r = xyqr(ids[0])
    j3 = q & 1
    s3 = pick(3, j3)
    for t, ref in enumerate((q_ref, k_ref, v_ref, u_ref)):
        lo = t * 128
        out_ref[0, lo : lo + 128] = ref[:, :D]
        out_ref[1, lo : lo + 128] = ref[:, D : 2 * D]
        out_ref[2, lo : lo + 64] = mm(s3, cols(ref, 2 + j3)).astype(BF)
        out_ref[2, lo + 64 : lo + 128] = g3_ref[t * 64 : (t + 1) * 64]
        for u in range(4):
            out_ref[3, lo + u * 32 : lo + u * 32 + 32] = qr_ref[u, t * 32 : (t + 1) * 32]


def attention(qs, ks, vs, us, docs, mult):
    nb = len(qs)
    keys, vals = jnp.concatenate(ks, 0), jnp.concatenate(vs, 0)
    doc_all = jnp.concatenate(docs, 0)
    outs, dqs, dk, dv, term = [], [], None, None, jnp.zeros((1, 1), F32)
    for b in range(nb):
        raw = mm_nt(qs[b], keys)
        allowed = mm_nt(docs[b], doc_all) > 0.5
        scores = jnp.where(allowed, raw * mult, -1e30)
        expo = jnp.exp(scores - jnp.max(scores, axis=1, keepdims=True))
        probs = expo * (1.0 / jnp.sum(expo, axis=1, keepdims=True))
        low = probs.astype(BF)
        att = mm(low, vals)
        delta = jnp.sum(us[b].astype(F32) * att, axis=1, keepdims=True)
        ds = probs * (mm_nt(us[b], vals) - delta)
        term += jnp.sum(jnp.sum(ds * raw, axis=1, keepdims=True), axis=0, keepdims=True)
        ds_low = ds.astype(BF)
        outs.append(att.astype(BF))
        dqs.append((mm(ds_low, keys) * mult).astype(BF))
        dk_b, dv_b = mm_tn(ds_low, qs[b]), mm_tn(low, us[b])
        dk, dv = (dk_b, dv_b) if dk is None else (dk + dk_b, dv + dv_b)
    dk = (dk * mult).astype(BF)
    dv = dv.astype(BF)
    part = lambda z: [z[b * 128 : (b + 1) * 128] for b in range(nb)]
    return outs, dqs, part(dk), part(dv), term * (1.0 / math.sqrt(D))


def doc_onehot(pos, bounds_ref):
    return onehot((pos >= bounds_ref[0:1]) & (pos < bounds_ref[1:2]))


def at_lane(term, head):
    return jnp.where(iota((1, 128), 1) == head, term, 0.0)


def near_kernel(ids, sharp, q_ref, k_ref, v_ref, u_ref, bounds_ref, g1_ref, z0_ref, own_ref, back_ref, terms_ref):
    dev = ids[0]
    x, y, q, r = xyqr(dev)
    row = iota((128, 128), 0)
    here = doc_onehot(dev * 128 + row, bounds_ref)
    there = doc_onehot((dev ^ 1) * 128 + row, bounds_ref)
    inv = 1.0 / math.sqrt(D)
    refs = (q_ref, k_ref, v_ref, u_ref)
    total = jnp.zeros((1, 128), F32)
    for h in range(2):
        blocks = [[ref[:, h * D : (h + 1) * D]] for ref in refs]
        *res, term = attention(*blocks, [here], sharp[h] * inv)
        for t in range(4):
            z0_ref[t * 128 : (t + 1) * 128, h * D : (h + 1) * D] = res[t][0]
        total += at_lane(term, h)
    h = 2 + (r & 1)
    blocks = [[cols(ref, h), g1_ref[t * 128 : (t + 1) * 128]] for t, ref in enumerate(refs)]
    *res, term = attention(*blocks, [here, there], sharp[h] * inv)
    for t in range(4):
        own_ref[t * 128 : (t + 1) * 128] = res[t][0]
        back_ref[t * 128 : (t + 1) * 128] = res[t][1]
    terms_ref[...] = jnp.broadcast_to(total + at_lane(term, h), (8, 128))


def pieces(v):
    hi = v.astype(BF).astype(F32)
    mid = (v - hi).astype(BF).astype(F32)
    lo = v - hi - mid
    row = iota((16, 128), 0)
    return jnp.where(row == 0, hi, jnp.where(row == 1, mid, jnp.where(row == 2, lo, 0.0))).astype(BF)


def total_of(blocks):
    acc = blocks[0].astype(F32)
    for b in blocks[1:]:
        acc += b.astype(F32)
    return jnp.sum(acc, axis=0, keepdims=True)


def task_kernel(ids, sharp, in_ref, bounds_ref, terms_ref, out_ref):
    x, y, q, r = xyqr(ids[0])
    m = iota((128, 128), 0)
    j4, j5 = q, y & 1
    near, r3 = r < 2, r == 2
    far = r == 3
    q3 = q == 3
    u_m = jnp.where(near, q, jnp.where(r3, q ^ (m >> 6), m >> 5))
    y_m = jnp.where(far & (q == 2), y ^ ((m >> 4) & 1), jnp.where(far & q3, jnp.where(y < 2, (m >> 3) & 3, (m >> 2) & 3), y))
    x_m = jnp.where(far & q3 & (y >= 2), (m >> 4) & 1, x)
    level = jnp.where(near, 2, jnp.where(r3, 3, jnp.where(q < 2, 4, jnp.where(q == 2, 5, jnp.where(y < 2, 6, 7)))))
    j = jnp.where(near, r, jnp.where(r3, q & 1, jnp.where(q < 2, q, jnp.where(q == 2, y & 1, jnp.where(y < 2, y, x)))))
    sh = level - 2
    dil = jnp.left_shift(1, sh)
    offset = (5 + j * (dil >> 1)) & (dil - 1)
    i_m = m & (jnp.right_shift(128, sh) - 1)
    low = (x_m * 64 + y_m * 16 + u_m * 4) * 128 + i_m * dil + offset
    docs = [doc_onehot(low + s * 128, bounds_ref) for s in range(4)]
    head = level * 2 + j
    blocks = [[in_ref[s, t * 128 : (t + 1) * 128] for s in range(4)] for t in range(4)]
    *res, term = attention(*blocks, docs, sharp[head] * (1.0 / math.sqrt(D)))
    for s in range(4):
        for t in range(4):
            out_ref[s, t * 128 : (t + 1) * 128] = res[t][s]
    extra = pieces(terms_ref[0:1] + at_lane(term, head))
    for s in range(4):
        out_ref[s, 512:528] = extra


def from_r_kernel(in_ref, g3_ref, out_ref):
    for t in range(4):
        g3_ref[t * 64 : (t + 1) * 64] = in_ref[2, t * 128 + 64 : t * 128 + 128]
        for u in range(4):
            out_ref[u, t * 32 : (t + 1) * 32] = in_ref[3, t * 128 + u * 32 : t * 128 + u * 32 + 32]
    extra = pieces(total_of([in_ref[s, 512:528] for s in range(4)]))
    for u in range(4):
        out_ref[u, 128:144] = extra


def from_q_kernel(ids, in_ref, g5_ref, out_ref):
    x, y, q, r = xyqr(ids[0])
    for t in range(4):
        g5_ref[t * 16 : (t + 1) * 16] = in_ref[2, t * 32 + 16 : t * 32 + 32]
    want = xy_col(x, y, iota((256, 128), 1))
    perm = onehot(want == iota((256, 128), 0))
    rows = mm(perm, in_ref[3, 0:128]).astype(BF)
    extra = pieces(total_of([in_ref[s, 128:144] for s in range(4)]))
    for d in range(8):
        out_ref[d, 0:32] = rows[d * 32 : (d + 1) * 32]
        out_ref[d, 32:48] = extra


def sum_kernel(in_ref, out_ref):
    out_ref[...] = jnp.broadcast_to(total_of([in_ref[s, 32:48] for s in range(8)]), (8, 128))


def unpack_kernel(ids, z0_ref, own_ref, g1_ref, rr_ref, g3_ref, qr_ref, g5_ref, xy_ref, o_ref, dq_ref, dk_ref, dv_ref):
    x, y, q, r = xyqr(ids[0])

    def spread(level, j):
        n = 128 // DIL[level]
        return onehot(iota((128, n), 0) == iota((128, n), 1) * DIL[level] + off(level, j))

    def put(ref, head, value):
        ref[:, pl.ds(pl.multiple_of(head * D, D), D)] = value.astype(BF)

    j1, j3, j5 = r & 1, q & 1, y & 1
    w3, w3b = spread(3, j3), spread(3, 1 - j3)
    w40, w41 = spread(4, 0), spread(4, 1)
    w5, w5b = spread(5, j5), spread(5, 1 - j5)
    pi, ci = iota((128, 32), 0), iota((128, 32), 1)
    for t, ref in enumerate((o_ref, dq_ref, dk_ref, dv_ref)):
        lo = t * 128
        ref[:, : 2 * D] = z0_ref[lo : lo + 128]
        put(ref, 2 + j1, own_ref[lo : lo + 128])
        put(ref, 3 - j1, g1_ref[lo : lo + 128])
        ref[:, 4 * D : 5 * D] = rr_ref[0, lo : lo + 128]
        ref[:, 5 * D : 6 * D] = rr_ref[1, lo : lo + 128]
        put(ref, 6 + j3, mm(w3, rr_ref[2, lo : lo + 64]))
        put(ref, 7 - j3, mm(w3b, g3_ref[t * 64 : (t + 1) * 64]))
        put(ref, 8, mm(w40, qr_ref[0, t * 32 : (t + 1) * 32]))
        put(ref, 9, mm(w41, qr_ref[1, t * 32 : (t + 1) * 32]))
        put(ref, 10 + j5, mm(w5, qr_ref[2, t * 32 : t * 32 + 16]))
        put(ref, 11 - j5, mm(w5b, g5_ref[t * 16 : (t + 1) * 16]))
        for j in range(2):
            w6 = onehot(pi == (ci - t * 8) * 16 + off(6, j))
            w7 = onehot(pi == (ci - t * 4) * 32 + off(7, j))
            put(ref, 12 + j, mm(w6, xy_ref[x * 4 + j, 0:32]))
            put(ref, 14 + j, mm(w7, xy_ref[j * 4 + 2, 0:32]))


SMEM = pl.BlockSpec(memory_space=pltpu.SMEM)
VMEM = pl.BlockSpec(memory_space=pltpu.VMEM)


def heads(first, count):
    return pl.BlockSpec((128, count * D), lambda i: (0, first // count))


def whole(array):
    return pl.BlockSpec(array.shape, lambda i: (0,) * len(array.shape))


def call(kernel, outs, scalars, sliced, rest, name):
    shapes = [jax.ShapeDtypeStruct(s, d) for s, d in outs]
    single = len(shapes) == 1
    specs = [pl.BlockSpec(s.shape, lambda i, n=len(s.shape): (0,) * n) for s in shapes]
    return pl.pallas_call(
        kernel,
        grid=(1,),
        in_specs=[SMEM] * len(scalars) + [heads(f, c) for _, f, c in sliced] + [whole(a) for a in rest],
        out_specs=specs[0] if single else specs,
        out_shape=shapes[0] if single else shapes,
        name=name,
    )(*scalars, *[a for a, _, _ in sliced], *rest)


def xor_pairs(n, v):
    return [(i, i ^ v) for i in range(n)]


def body(asking_vectors, lookup_vectors, payload_vectors, incoming_sensitivity, learned_sharpness, reply_list_sizes):
    four = [a[0] for a in (asking_vectors, lookup_vectors, payload_vectors, incoming_sensitivity)]
    ids = lax.axis_index(SEQ).astype(jnp.int32).reshape(1)
    ends = jnp.cumsum(reply_list_sizes[0])
    n_docs = ends.shape[0]
    starts = jnp.concatenate([jnp.zeros((1,), jnp.int32), ends[:-1]])
    ends = jnp.concatenate([ends[:-1], jnp.full((1,), 1 << 30, jnp.int32)])
    bounds = jnp.pad(jnp.stack([starts, ends]), ((0, 6), (0, 128 - n_docs)))

    g1, g3, g5, xy = call(
        pack_kernel,
        [((512, D), BF), ((256, D), BF), ((64, D), BF), ((8, 32, D), BF)],
        [ids], [(a, 0, 16) for a in four], [], "pack",
    )
    g3 = lax.ppermute(g3, "q", xor_pairs(4, 1))
    g5 = lax.ppermute(g5, "y", xor_pairs(4, 1))
    g1 = lax.ppermute(g1, "r", xor_pairs(4, 1))
    xy = lax.all_to_all(xy, ("x", "y"), 0, 0)
    qs = call(to_q_kernel, [((4, 128, D), BF)], [ids], [(a, 8, 4) for a in four], [g5, xy], "to_q")
    qs = lax.all_to_all(qs, "q", 0, 0)
    rs = call(to_r_kernel, [((4, 512, D), BF)], [ids], [(a, 4, 4) for a in four], [g3, qs], "to_r")
    z0, own1, back1, terms = call(
        near_kernel,
        [((512, 2 * D), BF), ((512, D), BF), ((512, D), BF), ((8, 128), F32)],
        [ids, learned_sharpness], [(a, 0, 4) for a in four], [bounds, g1], "near",
    )
    back1 = lax.ppermute(back1, "r", xor_pairs(4, 1))
    rs = lax.all_to_all(rs, "r", 0, 0)
    rs = call(task_kernel, [((4, 528, D), BF)], [ids, learned_sharpness], [], [rs, bounds, terms], "task")
    rs = lax.all_to_all(rs, "r", 0, 0)
    back3, qs = call(from_r_kernel, [((256, D), BF), ((4, 144, D), BF)], [], [], [rs], "from_r")
    back3 = lax.ppermute(back3, "q", xor_pairs(4, 1))
    qs = lax.all_to_all(qs, "q", 0, 0)
    back5, xy = call(from_q_kernel, [((64, D), BF), ((8, 48, D), BF)], [ids], [], [qs], "from_q")
    back5 = lax.ppermute(back5, "y", xor_pairs(4, 1))
    xy = lax.all_to_all(xy, ("x", "y"), 0, 0)
    terms = call(sum_kernel, [((8, 128), F32)], [], [], [xy], "scale_sum")
    parts = [lax.ppermute(terms, "dp", xor_pairs(4, v)) for v in (1, 2, 3)]
    outs = call(
        unpack_kernel, [((128, 16 * D), BF)] * 4, [ids], [],
        [z0, own1, back1, rs, back3, qs, back5, xy], "unpack",
    )
    scale_gradient = ((terms + parts[0]) + (parts[1] + parts[2]))[0, :16]
    return (*[o[None] for o in outs], scale_gradient)


def solution(mesh):
    fine = Mesh(mesh.devices.reshape(2, 4, 4, 4, 4), SEQ + ("dp",))
    rows = P("dp", SEQ, None)
    in_specs = (rows, rows, rows, rows, P(), P("dp", None))
    out_specs = (rows, rows, rows, rows, P())
    return jax.shard_map(body, mesh=fine, in_specs=in_specs, out_specs=out_specs, check_vma=False)
```

```python
import math

import jax
import jax.numpy as jnp
from jax import lax
from jax.experimental import pallas as pl
from jax.experimental.pallas import tpu as pltpu
from jax.sharding import Mesh, PartitionSpec as P

D = 128
BF = jnp.bfloat16
F32 = jnp.float32
DIL = (1, 1, 1, 2, 4, 8, 16, 32)
SEQ = ("x", "y", "q", "r")


def off(level, j):
    dil = DIL[level]
    return (5 + j * (dil // 2)) % dil


def iota(shape, dim):
    return lax.broadcasted_iota(jnp.int32, shape, dim)


def onehot(cond):
    return cond.astype(F32).astype(BF)


def mm(a, b):
    return jnp.dot(a, b, preferred_element_type=F32)


def mm_nt(a, b):
    return lax.dot_general(a, b, (((1,), (1,)), ((), ())), preferred_element_type=F32)


def mm_tn(a, b):
    return lax.dot_general(a, b, (((0,), (0,)), ((), ())), preferred_element_type=F32)


def pick(level, j, rows=128):
    n = 128 // DIL[level]
    return onehot(iota((n, 128), 1) == iota((n, 128), 0) * DIL[level] + off(level, j))


def cols(ref, head, first=0):
    return ref[:, pl.ds(pl.multiple_of((head - first) * D, D), D)]


def xyqr(dev):
    return dev >> 6, (dev >> 4) & 3, (dev >> 2) & 3, dev & 3


def xy_col(x, y, row):
    t, m = row >> 5, row & 31
    six = (x * 4 + (m >> 3)) * 32 + t * 8 + (m & 7)
    seven = (m >> 2) * 32 + t * 4 + (m & 3)
    return jnp.where(y < 2, six, jnp.where(y == 2, seven, -1))


def pack_kernel(ids, q_ref, k_ref, v_ref, u_ref, xy_ref):
    x, y, q, r = xyqr(ids[0])
    srcs = (q_ref, k_ref, v_ref, u_ref)
    j5 = 1 - (y & 1)
    s5 = pick(5, j5)
    xy_ref[...] = jnp.zeros(xy_ref.shape, BF)
    for t, ref in enumerate(srcs):
        xy_ref[x * 4 + (y ^ 1), 32 + t * 16 : 48 + t * 16] = mm(s5, cols(ref, 2 + j5)).astype(BF)
    for j in range(2):
        acc6 = jnp.zeros((32, D), F32)
        acc7 = jnp.zeros((32, D), F32)
        ri, ci = iota((32, 128), 0), iota((32, 128), 1)
        for t, ref in enumerate(srcs):
            w6 = onehot((ci == (ri - t * 8) * 16 + off(6, j)))
            w7 = onehot((ci == (ri - t * 4) * 32 + off(7, j)))
            acc6 += mm(w6, ref[:, (4 + j) * D : (5 + j) * D])
            acc7 += mm(w7, ref[:, (6 + j) * D : (7 + j) * D])
        xy_ref[x * 4 + j, 0:32] = acc6.astype(BF)
        xy_ref[j * 4 + 2, 0:32] = acc7.astype(BF)


def pairs_kernel(ids, q_ref, k_ref, v_ref, u_ref, g3_ref):
    x, y, q, r = xyqr(ids[0])
    j3 = 1 - (q & 1)
    s3 = pick(3, j3)
    for t, ref in enumerate((q_ref, k_ref, v_ref, u_ref)):
        g3_ref[t * 64 : (t + 1) * 64] = mm(s3, cols(ref, 6 + j3)).astype(BF)


def to_q_kernel(ids, q_ref, k_ref, v_ref, u_ref, xy_ref, own_ref, s1_ref, s2_ref, s3_ref, tmp):
    x, y, q, r = xyqr(ids[0])
    j5 = y & 1
    s40, s41, s5 = pick(4, 0), pick(4, 1), pick(5, j5)
    for t, ref in enumerate((q_ref, k_ref, v_ref, u_ref)):
        tmp[0, t * 32 : (t + 1) * 32] = mm(s40, ref[:, 8 * D : 9 * D]).astype(BF)
        tmp[1, t * 32 : (t + 1) * 32] = mm(s41, ref[:, 9 * D : 10 * D]).astype(BF)
        tmp[2, t * 32 : t * 32 + 16] = mm(s5, cols(ref, 10 + j5)).astype(BF)
        tmp[2, t * 32 + 16 : t * 32 + 32] = xy_ref[x * 4 + (y ^ 1), 32 + t * 16 : 48 + t * 16]
    want = xy_col(x, y, iota((128, 256), 0))
    perm = onehot(want == iota((128, 256), 1))
    tmp[3] = mm(perm, xy_ref[:, 0:32].reshape(256, D)).astype(BF)
    for v, ref in enumerate((own_ref, s1_ref, s2_ref, s3_ref)):
        ref[...] = tmp[q ^ v]


def to_r_kernel(ids, q_ref, k_ref, v_ref, u_ref, g3_ref, q0, q1, q2, q3, own_ref, t1_ref, t2_ref, t3_ref, tmp):
    x, y, q, r = xyqr(ids[0])
    j3 = q & 1
    h1 = 3 - (r & 1)
    s3 = pick(3, j3)
    for t, ref in enumerate((q_ref, k_ref, v_ref, u_ref)):
        lo = t * 128
        tmp[0, lo : lo + 128] = ref[:, 4 * D : 5 * D]
        tmp[1, lo : lo + 128] = ref[:, 5 * D : 6 * D]
        tmp[2, lo : lo + 64] = mm(s3, cols(ref, 6 + j3)).astype(BF)
        tmp[2, lo + 64 : lo + 128] = g3_ref[t * 64 : (t + 1) * 64]
        for v, src in enumerate((q0, q1, q2, q3)):
            tmp[3, lo + v * 32 : lo + v * 32 + 32] = src[t * 32 : (t + 1) * 32]
        t1_ref[512 + lo : 640 + lo] = cols(ref, h1)
    for v, ref in enumerate((own_ref, t1_ref, t2_ref, t3_ref)):
        ref[0:512] = tmp[r ^ v]


def attention(qs, ks, vs, us, docs, mult):
    nb = len(qs)
    keys, vals = jnp.concatenate(ks, 0), jnp.concatenate(vs, 0)
    doc_all = jnp.concatenate(docs, 0)
    outs, dqs, dk, dv, term = [], [], None, None, jnp.zeros((1, 1), F32)
    for b in range(nb):
        raw = mm_nt(qs[b], keys)
        allowed = mm_nt(docs[b], doc_all) > 0.5
        scores = jnp.where(allowed, raw * mult, -1e30)
        expo = jnp.exp(scores - jnp.max(scores, axis=1, keepdims=True))
        probs = expo * (1.0 / jnp.sum(expo, axis=1, keepdims=True))
        low = probs.astype(BF)
        att = mm(low, vals)
        delta = jnp.sum(us[b].astype(F32) * att, axis=1, keepdims=True)
        ds = probs * (mm_nt(us[b], vals) - delta)
        term += jnp.sum(jnp.sum(ds * raw, axis=1, keepdims=True), axis=0, keepdims=True)
        ds_low = ds.astype(BF)
        outs.append(att.astype(BF))
        dqs.append((mm(ds_low, keys) * mult).astype(BF))
        dk_b, dv_b = mm_tn(ds_low, qs[b]), mm_tn(low, us[b])
        dk, dv = (dk_b, dv_b) if dk is None else (dk + dk_b, dv + dv_b)
    dk = (dk * mult).astype(BF)
    dv = dv.astype(BF)
    part = lambda z: [z[b * 128 : (b + 1) * 128] for b in range(nb)]
    return outs, dqs, part(dk), part(dv), term * (1.0 / math.sqrt(D))


def doc_onehot(pos, bounds_ref):
    return onehot((pos >= bounds_ref[0:1]) & (pos < bounds_ref[1:2]))


def at_lane(term, head):
    return jnp.where(iota((1, 128), 1) == head, term, 0.0)


def near_kernel(ids, sharp, q_ref, k_ref, v_ref, u_ref, bounds_ref, g1_ref, z0_ref, own_ref, back_ref, terms_ref):
    dev = ids[0]
    x, y, q, r = xyqr(dev)
    row = iota((128, 128), 0)
    here = doc_onehot(dev * 128 + row, bounds_ref)
    there = doc_onehot((dev ^ 1) * 128 + row, bounds_ref)
    inv = 1.0 / math.sqrt(D)
    refs = (q_ref, k_ref, v_ref, u_ref)
    total = jnp.zeros((1, 128), F32)
    for h in range(2):
        blocks = [[ref[:, h * D : (h + 1) * D]] for ref in refs]
        *res, term = attention(*blocks, [here], sharp[h] * inv)
        for t in range(4):
            z0_ref[t * 128 : (t + 1) * 128, h * D : (h + 1) * D] = res[t][0]
        total += at_lane(term, h)
    h = 2 + (r & 1)
    blocks = [[cols(ref, h), g1_ref[512 + t * 128 : 640 + t * 128]] for t, ref in enumerate(refs)]
    *res, term = attention(*blocks, [here, there], sharp[h] * inv)
    for t in range(4):
        own_ref[t * 128 : (t + 1) * 128] = res[t][0]
        back_ref[t * 128 : (t + 1) * 128] = res[t][1]
    terms_ref[...] = jnp.broadcast_to(total + at_lane(term, h), (8, 128))


def pieces(v):
    hi = v.astype(BF).astype(F32)
    mid = (v - hi).astype(BF).astype(F32)
    lo = v - hi - mid
    row = iota((16, 128), 0)
    return jnp.where(row == 0, hi, jnp.where(row == 1, mid, jnp.where(row == 2, lo, 0.0))).astype(BF)


def task_kernel(ids, sharp, i0, i1, i2, i3, bounds_ref, terms_ref, back_ref, o0, o1, o2, o3):
    ins, outs = (i0, i1, i2, i3), (o0, o1, o2, o3)
    x, y, q, r = xyqr(ids[0])
    m = iota((128, 128), 0)
    j4, j5 = q, y & 1
    near, r3 = r < 2, r == 2
    far = r == 3
    q3 = q == 3
    u_m = jnp.where(near, q, q ^ jnp.where(r3, m >> 6, m >> 5))
    y_m = jnp.where(far & (q == 2), y ^ ((m >> 4) & 1), jnp.where(far & q3, jnp.where(y < 2, (m >> 3) & 3, (m >> 2) & 3), y))
    x_m = jnp.where(far & q3 & (y >= 2), (m >> 4) & 1, x)
    level = jnp.where(near, 2, jnp.where(r3, 3, jnp.where(q < 2, 4, jnp.where(q == 2, 5, jnp.where(y < 2, 6, 7)))))
    j = jnp.where(near, r, jnp.where(r3, q & 1, jnp.where(q < 2, q, jnp.where(q == 2, y & 1, jnp.where(y < 2, y, x)))))
    sh = level - 2
    dil = jnp.left_shift(1, sh)
    offset = (5 + j * (dil >> 1)) & (dil - 1)
    i_m = m & (jnp.right_shift(128, sh) - 1)
    low = (x_m * 64 + y_m * 16 + u_m * 4) * 128 + i_m * dil + offset
    docs = [doc_onehot(low + (r ^ v) * 128, bounds_ref) for v in range(4)]
    head = level * 2 + j
    blocks = [[ref[t * 128 : (t + 1) * 128] for ref in ins] for t in range(4)]
    *res, term = attention(*blocks, docs, sharp[head] * (1.0 / math.sqrt(D)))
    extra = pieces(terms_ref[0:1] + at_lane(term, head))
    for v, ref in enumerate(outs):
        for t in range(4):
            ref[t * 128 : (t + 1) * 128] = res[t][v]
        ref[512:528] = extra
    o1[528:1040] = back_ref[...]


def total4(blocks):
    a, b, c, d = [jnp.sum(z.astype(F32), axis=0, keepdims=True) for z in blocks]
    return (a + b) + (c + d)


def from_r_kernel(ids, i0, i1, i2, i3, own_ref, p1_ref, p2_ref, p3_ref):
    x, y, q, r = xyqr(ids[0])
    ins, outs = (i0, i1, i2, i3), (own_ref, p1_ref, p2_ref, p3_ref)
    for v, ref in enumerate(ins):

        @pl.when((r ^ v) == 2)
        def _():
            for t in range(4):
                p1_ref[144 + t * 64 : 208 + t * 64] = ref[t * 128 + 64 : t * 128 + 128]

        @pl.when((r ^ v) == 3)
        def _():
            for t in range(4):
                for w, out in enumerate(outs):
                    out[t * 32 : (t + 1) * 32] = ref[t * 128 + w * 32 : t * 128 + w * 32 + 32]

    extra = pieces(total4([ref[512:528] for ref in ins]))
    for out in outs:
        out[128:144] = extra


def from_q_kernel(ids, i0, i1, i2, i3, g5_ref, out_ref):
    x, y, q, r = xyqr(ids[0])
    dp = ids[1]
    ins = (i0, i1, i2, i3)
    want = xy_col(x, y, iota((256, 128), 1))
    perm = onehot(want == iota((256, 128), 0))
    extra = pieces(total4([ref[128:144] for ref in ins]))
    for d in range(32):
        out_ref[d, 0:32] = jnp.zeros((32, D), BF)
        out_ref[d, 32:48] = extra
    for v, ref in enumerate(ins):

        @pl.when((q ^ v) == 2)
        def _():
            for t in range(4):
                g5_ref[t * 16 : (t + 1) * 16] = ref[t * 32 + 16 : t * 32 + 32]

        @pl.when((q ^ v) == 3)
        def _():
            rows = mm(perm, ref[0:128]).astype(BF)
            for d in range(8):
                out_ref[d * 4 + dp, 0:32] = rows[d * 32 : (d + 1) * 32]


def spread(level, j):
    n = 128 // DIL[level]
    return onehot(iota((128, n), 0) == iota((128, n), 1) * DIL[level] + off(level, j))


def put(ref, head, value):
    ref[:, pl.ds(pl.multiple_of(head * D, D), D)] = value.astype(BF)


def unpack_low_kernel(ids, z0_ref, own_ref, r0, r1, r2, r3, q1, o_ref, dq_ref, dk_ref, dv_ref):
    x, y, q, r = xyqr(ids[0])
    res = (o_ref, dq_ref, dk_ref, dv_ref)
    j1, j3 = r & 1, q & 1
    w3b = spread(3, 1 - j3)
    for t, ref in enumerate(res):
        lo = t * 128
        ref[:, : 2 * D] = z0_ref[lo : lo + 128]
        put(ref, 2 + j1, own_ref[lo : lo + 128])
        put(ref, 3 - j1, r1[528 + lo : 656 + lo])
        put(ref, 7 - j3, mm(w3b, q1[144 + t * 64 : 208 + t * 64]))
    for v, src in enumerate((r0, r1, r2, r3)):
        role = r ^ v

        @pl.when(role < 2)
        def _():
            for t, ref in enumerate(res):
                put(ref, 4 + role, src[t * 128 : (t + 1) * 128])

        @pl.when(role == 2)
        def _():
            w3 = spread(3, j3)
            for t, ref in enumerate(res):
                put(ref, 6 + j3, mm(w3, src[t * 128 : t * 128 + 64]))


def unpack_high_kernel(ids, l0, l1, l2, l3, q0, q1, q2, q3, g5_ref, xy_ref, o_ref, dq_ref, dk_ref, dv_ref, terms_ref):
    x, y, q, r = xyqr(ids[0])
    dp = ids[1]
    res = (o_ref, dq_ref, dk_ref, dv_ref)
    j5 = y & 1
    w5b = spread(5, 1 - j5)
    pi, ci = iota((128, 32), 0), iota((128, 32), 1)
    for t, ref in enumerate(res):
        put(ref, 3 - j5, mm(w5b, g5_ref[t * 16 : (t + 1) * 16]))
        for j in range(2):
            w6 = onehot(pi == (ci - t * 8) * 16 + off(6, j))
            w7 = onehot(pi == (ci - t * 4) * 32 + off(7, j))
            put(ref, 4 + j, mm(w6, xy_ref[(x * 4 + j) * 4 + dp, 0:32]))
            put(ref, 6 + j, mm(w7, xy_ref[(j * 4 + 2) * 4 + dp, 0:32]))
    for v, src in enumerate((q0, q1, q2, q3)):
        role = q ^ v

        @pl.when(role < 2)
        def _():
            w4 = spread(4, role)
            for t, ref in enumerate(res):
                put(ref, role, mm(w4, src[t * 32 : (t + 1) * 32]))

        @pl.when(role == 2)
        def _():
            w5 = spread(5, j5)
            for t, ref in enumerate(res):
                put(ref, 2 + j5, mm(w5, src[t * 32 : t * 32 + 16]))

    acc = xy_ref[0, 32:48].astype(F32)
    for d in range(1, 32):
        acc += xy_ref[d, 32:48].astype(F32)
    terms_ref[...] = jnp.broadcast_to(jnp.sum(acc, axis=0, keepdims=True), (8, 128))


SMEM = pl.BlockSpec(memory_space=pltpu.SMEM)
VMEM = pl.BlockSpec(memory_space=pltpu.VMEM)
LIMIT = pltpu.CompilerParams(vmem_limit_bytes=20 << 20)


def stay(array):
    return pltpu.with_memory_space_constraint(array, pltpu.VMEM)


def call(kernel, outs, scalars, params, rest, name, scratch=(), out_space=pltpu.VMEM):
    shapes = [out_space(s, d) for s, d in outs]
    single = len(shapes) == 1
    return pl.pallas_call(
        kernel,
        in_specs=[SMEM] * len(scalars) + [VMEM] * (len(params) + len(rest)),
        out_specs=VMEM if single else [VMEM] * len(shapes),
        out_shape=shapes[0] if single else shapes,
        scratch_shapes=list(scratch),
        compiler_params=LIMIT,
        name=name,
    )(*scalars, *params, *[stay(a) for a in rest])


def swap(array, axis, v):
    return lax.ppermute(array, axis, [(i, i ^ v) for i in range(4)])


def body(asking_vectors, lookup_vectors, payload_vectors, incoming_sensitivity, learned_sharpness, reply_list_sizes):
    raw = [a[0] for a in (asking_vectors, lookup_vectors, payload_vectors, incoming_sensitivity)]
    ids = jnp.stack([lax.axis_index(SEQ), lax.axis_index("dp")]).astype(jnp.int32)
    block = lambda n: ((n, D), BF)
    xy = pl.pallas_call(
        pack_kernel,
        grid=(1,),
        in_specs=[SMEM] + [pl.BlockSpec((128, 8 * D), lambda i: (0, 1))] * 4,
        out_specs=pl.BlockSpec((8, 96, D), lambda i: (0, 0, 0)),
        out_shape=jax.ShapeDtypeStruct((8, 96, D), BF),
        compiler_params=LIMIT,
        name="pack",
    )(ids, *raw)
    xy = lax.all_to_all(xy, ("x", "y"), 0, 0)
    four = [stay(a) for a in raw]
    ends = jnp.cumsum(reply_list_sizes[0])
    n_docs = ends.shape[0]
    starts = jnp.concatenate([jnp.zeros((1,), jnp.int32), ends[:-1]])
    ends = jnp.concatenate([ends[:-1], jnp.full((1,), 1 << 30, jnp.int32)])
    bounds = jnp.pad(jnp.stack([starts, ends]), ((0, 6), (0, 128 - n_docs)))

    g3 = swap(call(pairs_kernel, [block(256)], [ids], four, [], "pairs"), "q", 1)
    q0, q1, q2, q3 = call(
        to_q_kernel, [block(128)] * 4, [ids], four, [xy], "to_q", [pltpu.VMEM((4, 128, D), BF)]
    )
    q2, q1, q3 = swap(q2, "q", 2), swap(q1, "q", 1), swap(q3, "q", 3)
    r0, r1, r2, r3 = call(
        to_r_kernel, [block(512), block(1024), block(512), block(512)], [ids], four, [g3, q0, q1, q2, q3], "to_r",
        [pltpu.VMEM((4, 512, D), BF)],
    )
    r1, r3, r2 = swap(r1, "r", 1), swap(r3, "r", 3), swap(r2, "r", 2)
    z0, own1, back1, terms = call(
        near_kernel,
        [((512, 2 * D), BF), block(512), block(512), ((8, 128), F32)],
        [ids, learned_sharpness], four, [bounds, r1], "near",
    )
    r0, r1, r2, r3 = call(
        task_kernel, [block(528), block(1040), block(528), block(528)], [ids, learned_sharpness], [],
        [r0, r1, r2, r3, bounds, terms, back1], "task",
    )
    r3, r2, r1 = swap(r3, "r", 3), swap(r2, "r", 2), swap(r1, "r", 1)
    q0, q1, q2, q3 = call(
        from_r_kernel, [block(144), block(400), block(144), block(144)], [ids], [], [r0, r1, r2, r3], "from_r"
    )
    q2, q1, q3 = swap(q2, "q", 2), swap(q1, "q", 1), swap(q3, "q", 3)
    back5, xy = call(from_q_kernel, [block(64), ((32, 48, D), BF)], [ids], [], [q0, q1, q2, q3], "from_q")
    xy = lax.all_to_all(xy, ("x", "y", "dp"), 0, 0)
    back5 = swap(back5, "y", 1)
    half = lambda i: pl.BlockSpec((128, 8 * D), lambda _: (0, i))
    result = jax.ShapeDtypeStruct((128, 16 * D), BF)
    args = [z0, own1, r0, r1, r2, r3, q1]
    outs = pl.pallas_call(
        unpack_low_kernel,
        grid=(1,),
        in_specs=[SMEM] + [VMEM] * len(args),
        out_specs=[half(0)] * 4,
        out_shape=[result] * 4,
        compiler_params=LIMIT,
        name="unpack_low",
    )(ids, *[stay(a) for a in args])
    args = [q0, q1, q2, q3, back5, xy]
    *outs, terms = pl.pallas_call(
        unpack_high_kernel,
        grid=(1,),
        in_specs=[SMEM] + [pl.BlockSpec(memory_space=pl.ANY)] * 4 + [VMEM] * len(args),
        out_specs=[half(1)] * 4 + [pl.BlockSpec((8, 128), lambda _: (0, 0))],
        out_shape=[result] * 4 + [jax.ShapeDtypeStruct((8, 128), F32)],
        input_output_aliases={1: 0, 2: 1, 3: 2, 4: 3},
        compiler_params=LIMIT,
        name="unpack_high",
    )(ids, *outs, *[stay(a) for a in args])
    return (*[o[None] for o in outs], terms[0, :16])


def solution(mesh):
    fine = Mesh(mesh.devices.reshape(2, 4, 4, 4, 4), SEQ + ("dp",))
    rows = P("dp", SEQ, None)
    in_specs = (rows, rows, rows, rows, P(), P("dp", None))
    out_specs = (rows, rows, rows, rows, P())
    return jax.shard_map(body, mesh=fine, in_specs=in_specs, out_specs=out_specs, check_vma=False)
```

```python
import math

import jax
import jax.numpy as jnp
from jax import lax
from jax.experimental import pallas as pl
from jax.experimental.pallas import tpu as pltpu
from jax.sharding import Mesh, PartitionSpec as P


D = 128
BF = jnp.bfloat16
F32 = jnp.float32
DIL = (1, 1, 1, 2, 4, 8, 16, 32)
SEQ = ("x", "y", "q", "r")


def off(level, j):
    dil = DIL[level]
    return (5 + j * (dil // 2)) % dil


def iota(shape, dim):
    return lax.broadcasted_iota(jnp.int32, shape, dim)


def onehot(cond):
    return cond.astype(F32).astype(BF)


def mm(a, b):
    return jnp.dot(a, b, preferred_element_type=F32)


def mm_nt(a, b):
    return lax.dot_general(a, b, (((1,), (1,)), ((), ())), preferred_element_type=F32)


def mm_tn(a, b):
    return lax.dot_general(a, b, (((0,), (0,)), ((), ())), preferred_element_type=F32)


def pick(level, j):
    n = 128 // DIL[level]
    return onehot(iota((n, 128), 1) == iota((n, 128), 0) * DIL[level] + off(level, j))


def cols(ref, head, first=0):
    return ref[:, pl.ds(pl.multiple_of((head - first) * D, D), D)]


def xyqr(dev):
    return dev >> 6, (dev >> 4) & 3, (dev >> 2) & 3, dev & 3


def xy_col(x, y, row):
    t, m = row >> 5, row & 31
    six = (x * 4 + (m >> 3)) * 32 + t * 8 + (m & 7)
    seven = (m >> 2) * 32 + t * 4 + (m & 3)
    return jnp.where(y < 2, six, jnp.where(y == 2, seven, -1))


def pack_kernel(ids, q_ref, k_ref, v_ref, u_ref, xy_ref):
    x, y, _, _ = xyqr(ids[0])
    srcs = (q_ref, k_ref, v_ref, u_ref)
    j5 = 1 - (y & 1)
    s5 = pick(5, j5)
    xy_ref[...] = jnp.zeros(xy_ref.shape, BF)
    for t, ref in enumerate(srcs):
        xy_ref[x * 4 + (y ^ 1), 32 + t * 16 : 48 + t * 16] = mm(s5, cols(ref, 2 + j5)).astype(BF)
    for j in range(2):
        acc6 = jnp.zeros((32, D), F32)
        acc7 = jnp.zeros((32, D), F32)
        ri, ci = iota((32, 128), 0), iota((32, 128), 1)
        for t, ref in enumerate(srcs):
            w6 = onehot((ci == (ri - t * 8) * 16 + off(6, j)))
            w7 = onehot((ci == (ri - t * 4) * 32 + off(7, j)))
            acc6 += mm(w6, ref[:, (4 + j) * D : (5 + j) * D])
            acc7 += mm(w7, ref[:, (6 + j) * D : (7 + j) * D])
        xy_ref[x * 4 + j, 0:32] = acc6.astype(BF)
        xy_ref[j * 4 + 2, 0:32] = acc7.astype(BF)


def to_q_kernel(ids, q_ref, k_ref, v_ref, u_ref, xy_ref, own_ref, s1_ref, s2_ref, s3_ref, tmp):
    x, y, q, _ = xyqr(ids[0])
    j3, j5 = 1 - (q & 1), y & 1
    s3, s40, s41, s5 = pick(3, j3), pick(4, 0), pick(4, 1), pick(5, j5)
    for t, ref in enumerate((q_ref, k_ref, v_ref, u_ref)):
        tmp[0, t * 32 : (t + 1) * 32] = mm(s40, ref[:, 8 * D : 9 * D]).astype(BF)
        tmp[1, t * 32 : (t + 1) * 32] = mm(s41, ref[:, 9 * D : 10 * D]).astype(BF)
        tmp[2, t * 32 : t * 32 + 16] = mm(s5, cols(ref, 10 + j5)).astype(BF)
        tmp[2, t * 32 + 16 : t * 32 + 32] = xy_ref[x * 4 + (y ^ 1), 32 + t * 16 : 48 + t * 16]
        s1_ref[128 + t * 64 : 192 + t * 64] = mm(s3, cols(ref, 6 + j3)).astype(BF)
    want = xy_col(x, y, iota((128, 256), 0))
    perm = onehot(want == iota((128, 256), 1))
    tmp[3] = mm(perm, xy_ref[:, 0:32].reshape(256, D)).astype(BF)
    for v, ref in enumerate((own_ref, s1_ref, s2_ref, s3_ref)):
        ref[0:128] = tmp[q ^ v]


def to_r_kernel(ids, q_ref, k_ref, v_ref, u_ref, q0, q1, q2, q3, own_ref, t1_ref, t2_ref, t3_ref, tmp):
    _, _, q, r = xyqr(ids[0])
    j3 = q & 1
    h1 = 3 - (r & 1)
    s3 = pick(3, j3)
    for t, ref in enumerate((q_ref, k_ref, v_ref, u_ref)):
        lo = t * 128
        tmp[0, lo : lo + 128] = ref[:, 4 * D : 5 * D]
        tmp[1, lo : lo + 128] = ref[:, 5 * D : 6 * D]
        tmp[2, lo : lo + 64] = mm(s3, cols(ref, 6 + j3)).astype(BF)
        tmp[2, lo + 64 : lo + 128] = q1[128 + t * 64 : 192 + t * 64]
        for v, src in enumerate((q0, q1, q2, q3)):
            tmp[3, lo + v * 32 : lo + v * 32 + 32] = src[t * 32 : (t + 1) * 32]
        t1_ref[512 + lo : 640 + lo] = cols(ref, h1)
    for v, ref in enumerate((own_ref, t1_ref, t2_ref, t3_ref)):
        ref[0:512] = tmp[r ^ v]


def attention(qs, ks, vs, us, docs, mult):
    nb = len(qs)
    keys, vals = jnp.concatenate(ks, 0), jnp.concatenate(vs, 0)
    doc_all = jnp.concatenate(docs, 0)
    outs, dqs, dk, dv, term = [], [], None, None, jnp.zeros((1, 1), F32)
    for b in range(nb):
        raw = mm_nt(qs[b], keys)
        allowed = mm_nt(docs[b], doc_all) > 0.5
        scores = jnp.where(allowed, raw * mult, -1e30)
        expo = jnp.exp(scores - jnp.max(scores, axis=1, keepdims=True))
        probs = expo * (1.0 / jnp.sum(expo, axis=1, keepdims=True))
        low = probs.astype(BF)
        att = mm(low, vals)
        delta = jnp.sum(us[b].astype(F32) * att, axis=1, keepdims=True)
        ds = probs * (mm_nt(us[b], vals) - delta)
        term += jnp.sum(jnp.sum(ds * raw, axis=1, keepdims=True), axis=0, keepdims=True)
        ds_low = ds.astype(BF)
        outs.append(att.astype(BF))
        dqs.append((mm(ds_low, keys) * mult).astype(BF))
        dk_b, dv_b = mm_tn(ds_low, qs[b]), mm_tn(low, us[b])
        dk, dv = (dk_b, dv_b) if dk is None else (dk + dk_b, dv + dv_b)
    dk = (dk * mult).astype(BF)
    dv = dv.astype(BF)
    part = lambda z: [z[b * 128 : (b + 1) * 128] for b in range(nb)]
    return outs, dqs, part(dk), part(dv), term * (1.0 / math.sqrt(D))


def doc_bounds(sizes):
    lane = iota((1, 128), 1)
    first, end = jnp.zeros((1, 128), jnp.int32), jnp.zeros((1, 128), jnp.int32)
    at = jnp.int32(0)
    for c in range(8):
        nxt = at + sizes[c] if c < 7 else jnp.int32(1 << 30)
        first, end = jnp.where(lane == c, at, first), jnp.where(lane == c, nxt, end)
        at = nxt
    return first, end


def doc_onehot(pos, bounds):
    return onehot((pos >= bounds[0]) & (pos < bounds[1]))


def at_lane(term, head):
    return jnp.where(iota((1, 128), 1) == head, term, 0.0)


def local_kernel(ids, sharp, sizes, q_ref, k_ref, v_ref, u_ref, z0_ref, terms_ref):
    here = doc_onehot(ids[0] * 128 + iota((128, 128), 0), doc_bounds(sizes))
    total = jnp.zeros((1, 128), F32)
    for h in range(2):
        blocks = [[ref[:, h * D : (h + 1) * D]] for ref in (q_ref, k_ref, v_ref, u_ref)]
        *res, term = attention(*blocks, [here], sharp[h] * (1.0 / math.sqrt(D)))
        for t in range(4):
            z0_ref[t * 128 : (t + 1) * 128, h * D : (h + 1) * D] = res[t][0]
        total += at_lane(term, h)
    terms_ref[...] = jnp.broadcast_to(total, (8, 128))


def near_kernel(ids, sharp, sizes, q_ref, k_ref, v_ref, u_ref, g1_ref, before_ref, own_ref, back_ref, terms_ref):
    dev = ids[0]
    _, _, _, r = xyqr(dev)
    row = iota((128, 128), 0)
    bounds = doc_bounds(sizes)
    here = doc_onehot(dev * 128 + row, bounds)
    there = doc_onehot((dev ^ 1) * 128 + row, bounds)
    refs = (q_ref, k_ref, v_ref, u_ref)
    h = 2 + (r & 1)
    blocks = [[cols(ref, h), g1_ref[512 + t * 128 : 640 + t * 128]] for t, ref in enumerate(refs)]
    *res, term = attention(*blocks, [here, there], sharp[h] * (1.0 / math.sqrt(D)))
    for t in range(4):
        own_ref[t * 128 : (t + 1) * 128] = res[t][0]
        back_ref[t * 128 : (t + 1) * 128] = res[t][1]
    terms_ref[...] = before_ref[...] + jnp.broadcast_to(at_lane(term, h), (8, 128))


def pieces(v):
    hi = v.astype(BF).astype(F32)
    mid = (v - hi).astype(BF).astype(F32)
    lo = v - hi - mid
    row = iota((16, 128), 0)
    return jnp.where(row == 0, hi, jnp.where(row == 1, mid, jnp.where(row == 2, lo, 0.0))).astype(BF)


def task_kernel(ids, sharp, sizes, i0, i1, i2, i3, terms_ref, back_ref, o0, o1, o2, o3):
    ins, outs = (i0, i1, i2, i3), (o0, o1, o2, o3)
    x, y, q, r = xyqr(ids[0])
    m = iota((128, 128), 0)
    near, r3 = r < 2, r == 2
    far = r == 3
    q3 = q == 3
    u_m = jnp.where(near, q, q ^ jnp.where(r3, m >> 6, m >> 5))
    y_m = jnp.where(far & (q == 2), y ^ ((m >> 4) & 1), jnp.where(far & q3, jnp.where(y < 2, (m >> 3) & 3, (m >> 2) & 3), y))
    x_m = jnp.where(far & q3 & (y >= 2), (m >> 4) & 1, x)
    level = jnp.where(near, 2, jnp.where(r3, 3, jnp.where(q < 2, 4, jnp.where(q == 2, 5, jnp.where(y < 2, 6, 7)))))
    j = jnp.where(near, r, jnp.where(r3, q & 1, jnp.where(q < 2, q, jnp.where(q == 2, y & 1, jnp.where(y < 2, y, x)))))
    sh = level - 2
    dil = jnp.left_shift(1, sh)
    offset = (5 + j * (dil >> 1)) & (dil - 1)
    i_m = m & (jnp.right_shift(128, sh) - 1)
    low = (x_m * 64 + y_m * 16 + u_m * 4) * 128 + i_m * dil + offset
    bounds = doc_bounds(sizes)
    docs = [doc_onehot(low + (r ^ v) * 128, bounds) for v in range(4)]
    head = level * 2 + j
    blocks = [[ref[t * 128 : (t + 1) * 128] for ref in ins] for t in range(4)]
    *res, term = attention(*blocks, docs, sharp[head] * (1.0 / math.sqrt(D)))
    extra = pieces(terms_ref[0:1] + at_lane(term, head))
    for v, ref in enumerate(outs):
        for t in range(4):
            ref[t * 128 : (t + 1) * 128] = res[t][v]
        ref[512:528] = extra
    o1[528:1040] = back_ref[...]


def total4(blocks):
    a, b, c, d = [jnp.sum(z.astype(F32), axis=0, keepdims=True) for z in blocks]
    return (a + b) + (c + d)


def from_r_kernel(ids, i0, i1, i2, i3, own_ref, p1_ref, p2_ref, p3_ref):
    _, _, _, r = xyqr(ids[0])
    ins, outs = (i0, i1, i2, i3), (own_ref, p1_ref, p2_ref, p3_ref)
    for v, ref in enumerate(ins):

        @pl.when((r ^ v) == 2)
        def _():
            for t in range(4):
                p1_ref[144 + t * 64 : 208 + t * 64] = ref[t * 128 + 64 : t * 128 + 128]

        @pl.when((r ^ v) == 3)
        def _():
            for t in range(4):
                for w, out in enumerate(outs):
                    out[t * 32 : (t + 1) * 32] = ref[t * 128 + w * 32 : t * 128 + w * 32 + 32]

    extra = pieces(total4([ref[512:528] for ref in ins]))
    for out in outs:
        out[128:144] = extra


def from_q_kernel(ids, i0, i1, i2, i3, g5_ref, out_ref):
    x, y, q, _ = xyqr(ids[0])
    dp = ids[1]
    ins = (i0, i1, i2, i3)
    want = xy_col(x, y, iota((256, 128), 1))
    perm = onehot(want == iota((256, 128), 0))
    extra = pieces(total4([ref[128:144] for ref in ins]))
    for d in range(32):
        out_ref[d, 0:32] = jnp.zeros((32, D), BF)
        out_ref[d, 32:48] = extra
    for v, ref in enumerate(ins):

        @pl.when((q ^ v) == 2)
        def _():
            for t in range(4):
                g5_ref[t * 16 : (t + 1) * 16] = ref[t * 32 + 16 : t * 32 + 32]

        @pl.when((q ^ v) == 3)
        def _():
            rows = mm(perm, ref[0:128]).astype(BF)
            for d in range(8):
                out_ref[d * 4 + dp, 0:32] = rows[d * 32 : (d + 1) * 32]


def spread(level, j):
    n = 128 // DIL[level]
    return onehot(iota((128, n), 0) == iota((128, n), 1) * DIL[level] + off(level, j))


def put(ref, head, value):
    ref[:, pl.ds(pl.multiple_of(head * D, D), D)] = value.astype(BF)


def unpack_low_kernel(ids, z0_ref, own_ref, r0, r1, r2, r3, q1, o_ref, dq_ref, dk_ref, dv_ref):
    _, _, q, r = xyqr(ids[0])
    res = (o_ref, dq_ref, dk_ref, dv_ref)
    j1, j3 = r & 1, q & 1
    w3b = spread(3, 1 - j3)
    for t, ref in enumerate(res):
        lo = t * 128
        ref[:, : 2 * D] = z0_ref[lo : lo + 128]
        put(ref, 2 + j1, own_ref[lo : lo + 128])
        put(ref, 3 - j1, r1[528 + lo : 656 + lo])
        put(ref, 7 - j3, mm(w3b, q1[144 + t * 64 : 208 + t * 64]))
    for v, src in enumerate((r0, r1, r2, r3)):
        role = r ^ v

        @pl.when(role < 2)
        def _():
            for t, ref in enumerate(res):
                put(ref, 4 + role, src[t * 128 : (t + 1) * 128])

        @pl.when(role == 2)
        def _():
            w3 = spread(3, j3)
            for t, ref in enumerate(res):
                put(ref, 6 + j3, mm(w3, src[t * 128 : t * 128 + 64]))


def unpack_high_kernel(ids, l0, l1, l2, l3, q0, q1, q2, q3, g5_ref, xy_ref, o_ref, dq_ref, dk_ref, dv_ref, terms_ref):
    x, y, q, _ = xyqr(ids[0])
    dp = ids[1]
    res = (o_ref, dq_ref, dk_ref, dv_ref)
    j5 = y & 1
    w5b = spread(5, 1 - j5)
    pi, ci = iota((128, 32), 0), iota((128, 32), 1)
    for t, ref in enumerate(res):
        put(ref, 3 - j5, mm(w5b, g5_ref[t * 16 : (t + 1) * 16]))
        for j in range(2):
            w6 = onehot(pi == (ci - t * 8) * 16 + off(6, j))
            w7 = onehot(pi == (ci - t * 4) * 32 + off(7, j))
            put(ref, 4 + j, mm(w6, xy_ref[(x * 4 + j) * 4 + dp, 0:32]))
            put(ref, 6 + j, mm(w7, xy_ref[(j * 4 + 2) * 4 + dp, 0:32]))
    for v, src in enumerate((q0, q1, q2, q3)):
        role = q ^ v

        @pl.when(role < 2)
        def _():
            w4 = spread(4, role)
            for t, ref in enumerate(res):
                put(ref, role, mm(w4, src[t * 32 : (t + 1) * 32]))

        @pl.when(role == 2)
        def _():
            w5 = spread(5, j5)
            for t, ref in enumerate(res):
                put(ref, 2 + j5, mm(w5, src[t * 32 : t * 32 + 16]))

    acc = xy_ref[0, 32:48].astype(F32)
    for d in range(1, 32):
        acc += xy_ref[d, 32:48].astype(F32)
    terms_ref[...] = jnp.sum(acc, axis=0, keepdims=True)[:, :16]


SMEM = pl.BlockSpec(memory_space=pltpu.SMEM)
VMEM = pl.BlockSpec(memory_space=pltpu.VMEM)
LIMIT = pltpu.CompilerParams(vmem_limit_bytes=20 << 20)


def stay(array):
    return pltpu.with_memory_space_constraint(array, pltpu.VMEM)


def call(kernel, outs, scalars, params, rest, scratch=(), out_space=pltpu.VMEM):
    shapes = [out_space(s, d) for s, d in outs]
    single = len(shapes) == 1
    run = pl.pallas_call(
        kernel,
        in_specs=[SMEM] * len(scalars) + [VMEM] * (len(params) + len(rest)),
        out_specs=VMEM if single else [VMEM] * len(shapes),
        out_shape=shapes[0] if single else shapes,
        scratch_shapes=list(scratch),
        compiler_params=LIMIT,
    )
    args = [*params, *[stay(a) for a in rest]]
    return run(*scalars, *args)


def swap(array, axis, v):
    return lax.ppermute(array, axis, [(i, i ^ v) for i in range(4)])


def body(asking_vectors, lookup_vectors, payload_vectors, incoming_sensitivity, learned_sharpness, reply_list_sizes):
    raw = [a[0] for a in (asking_vectors, lookup_vectors, payload_vectors, incoming_sensitivity)]
    ids = jnp.stack([lax.axis_index(SEQ), lax.axis_index("dp")]).astype(jnp.int32)
    block = lambda n: ((n, D), BF)
    xy = pl.pallas_call(
        pack_kernel,
        grid=(1,),
        in_specs=[SMEM] + [pl.BlockSpec((128, 8 * D), lambda i: (0, 1))] * 4,
        out_specs=pl.BlockSpec((8, 96, D), lambda i: (0, 0, 0)),
        out_shape=jax.ShapeDtypeStruct((8, 96, D), BF),
        compiler_params=LIMIT,
        name="pack",
    )(ids, *[pltpu.with_memory_space_constraint(a, pltpu.HBM) for a in raw])
    xy = lax.all_to_all(xy, ("x", "y"), 0, 0)
    four = [stay(a) for a in raw]
    sizes = reply_list_sizes[0]
    z0, terms = call(local_kernel, [((512, 2 * D), BF), ((8, 128), F32)], [ids, learned_sharpness, sizes], four, [])
    q0, q1, q2, q3 = call(
        to_q_kernel, [block(128), block(384), block(128), block(128)], [ids], four, [xy], [pltpu.VMEM((4, 128, D), BF)]
    )
    q2, q1, q3 = swap(q2, "q", 2), swap(q1, "q", 1), swap(q3, "q", 3)
    r0, r1, r2, r3 = call(
        to_r_kernel, [block(512), block(1024), block(512), block(512)], [ids], four, [q0, q1, q2, q3],
        [pltpu.VMEM((4, 512, D), BF)],
    )
    r1, r3, r2 = swap(r1, "r", 1), swap(r3, "r", 3), swap(r2, "r", 2)
    own1, back1, terms = call(
        near_kernel, [block(512), block(512), ((8, 128), F32)], [ids, learned_sharpness, sizes], four, [r1, terms]
    )
    r0, r1, r2, r3 = call(
        task_kernel, [block(528), block(1040), block(528), block(528)], [ids, learned_sharpness, sizes], [],
        [r0, r1, r2, r3, terms, back1],
    )
    r3, r2, r1 = swap(r3, "r", 3), swap(r2, "r", 2), swap(r1, "r", 1)
    q0, q1, q2, q3 = call(from_r_kernel, [block(144), block(400), block(144), block(144)], [ids], [], [r0, r1, r2, r3])
    q2, q1, q3 = swap(q2, "q", 2), swap(q1, "q", 1), swap(q3, "q", 3)
    back5, xy = call(from_q_kernel, [block(64), ((32, 48, D), BF)], [ids], [], [q0, q1, q2, q3])
    xy = lax.all_to_all(xy, ("x", "y", "dp"), 0, 0)
    back5 = swap(back5, "y", 1)
    half = lambda i: pl.BlockSpec((128, 8 * D), lambda _: (0, i))
    result = jax.ShapeDtypeStruct((128, 16 * D), BF)
    args = [z0, own1, r0, r1, r2, r3, q1]
    outs = pl.pallas_call(
        unpack_low_kernel,
        grid=(1,),
        in_specs=[SMEM] + [VMEM] * len(args),
        out_specs=[half(0)] * 4,
        out_shape=[result] * 4,
        compiler_params=LIMIT,
        name="unpack_low",
    )(ids, *[stay(a) for a in args])
    args = [q0, q1, q2, q3, back5, xy]
    *outs, terms = pl.pallas_call(
        unpack_high_kernel,
        grid=(1,),
        in_specs=[SMEM] + [pl.BlockSpec(memory_space=pl.ANY)] * 4 + [VMEM] * len(args),
        out_specs=[half(1)] * 4 + [pl.BlockSpec((1, 16), lambda _: (0, 0))],
        out_shape=[result] * 4 + [jax.ShapeDtypeStruct((1, 16), F32)],
        input_output_aliases={1: 0, 2: 1, 3: 2, 4: 3},
        compiler_params=LIMIT,
        name="unpack_high",
    )(ids, *outs, *[stay(a) for a in args])
    return (*[o[None] for o in outs], terms[0])


def solution(mesh):
    fine = Mesh(mesh.devices.reshape(2, 4, 4, 4, 4), SEQ + ("dp",))
    rows = P("dp", SEQ, None)
    in_specs = (rows, rows, rows, rows, P(), P("dp", None))
    out_specs = (rows, rows, rows, rows, P())
    return jax.shard_map(body, mesh=fine, in_specs=in_specs, out_specs=out_specs, check_vma=False)
```

```python
import math

import jax
import jax.numpy as jnp
from jax import lax
from jax.experimental import pallas as pl
from jax.experimental.pallas import tpu as pltpu
from jax.sharding import Mesh, PartitionSpec as P


D = 128
BF = jnp.bfloat16
F32 = jnp.float32
DIL = (1, 1, 1, 2, 4, 8, 16, 32)
SEQ = ("x", "y", "q", "r")


def off(level, j):
    dil = DIL[level]
    return (5 + j * (dil // 2)) % dil


def iota(shape, dim):
    return lax.broadcasted_iota(jnp.int32, shape, dim)


def onehot(cond):
    return cond.astype(F32).astype(BF)


def mm(a, b):
    return jnp.dot(a, b, preferred_element_type=F32)


def mm_nt(a, b):
    return lax.dot_general(a, b, (((1,), (1,)), ((), ())), preferred_element_type=F32)


def mm_tn(a, b):
    return lax.dot_general(a, b, (((0,), (0,)), ((), ())), preferred_element_type=F32)


def pick(level, j):
    n = 128 // DIL[level]
    return onehot(iota((n, 128), 1) == iota((n, 128), 0) * DIL[level] + off(level, j))


def cols(ref, head, first=0):
    return ref[:, pl.ds(pl.multiple_of((head - first) * D, D), D)]


def xyqr(dev):
    return dev >> 6, (dev >> 4) & 3, (dev >> 2) & 3, dev & 3


def xy_col(x, y, row):
    t, m = row >> 5, row & 31
    six = (x * 4 + (m >> 3)) * 32 + t * 8 + (m & 7)
    seven = (m >> 2) * 32 + t * 4 + (m & 3)
    return jnp.where(y < 2, six, jnp.where(y == 2, seven, -1))


def pack_kernel(ids, q6_ref, k6_ref, v6_ref, u6_ref, q_ref, k_ref, v_ref, u_ref, g3_ref, xy_ref):
    x, y, q, _ = xyqr(ids[0])
    srcs = (q_ref, k_ref, v_ref, u_ref)
    j5 = 1 - (y & 1)
    s5 = pick(5, j5)
    j3 = 1 - (q & 1)
    s3 = pick(3, j3)
    for t, ref in enumerate((q6_ref, k6_ref, v6_ref, u6_ref)):
        g3_ref[t * 64 : (t + 1) * 64] = mm(s3, cols(ref, j3)).astype(BF)
    xy_ref[...] = jnp.zeros(xy_ref.shape, BF)
    for t, ref in enumerate(srcs):
        xy_ref[x * 4 + (y ^ 1), 32 + t * 16 : 48 + t * 16] = mm(s5, cols(ref, 2 + j5)).astype(BF)
    for j in range(2):
        acc6 = jnp.zeros((32, D), F32)
        acc7 = jnp.zeros((32, D), F32)
        ri, ci = iota((32, 128), 0), iota((32, 128), 1)
        for t, ref in enumerate(srcs):
            w6 = onehot((ci == (ri - t * 8) * 16 + off(6, j)))
            w7 = onehot((ci == (ri - t * 4) * 32 + off(7, j)))
            acc6 += mm(w6, ref[:, (4 + j) * D : (5 + j) * D])
            acc7 += mm(w7, ref[:, (6 + j) * D : (7 + j) * D])
        xy_ref[x * 4 + j, 0:32] = acc6.astype(BF)
        xy_ref[j * 4 + 2, 0:32] = acc7.astype(BF)


def to_q_kernel(ids, q_ref, k_ref, v_ref, u_ref, xy_ref, out_ref):
    x, y, _, _ = xyqr(ids[0])
    j5 = y & 1
    s40, s41, s5 = pick(4, 0), pick(4, 1), pick(5, j5)
    for t, ref in enumerate((q_ref, k_ref, v_ref, u_ref)):
        out_ref[0, t * 32 : (t + 1) * 32] = mm(s40, ref[:, 8 * D : 9 * D]).astype(BF)
        out_ref[1, t * 32 : (t + 1) * 32] = mm(s41, ref[:, 9 * D : 10 * D]).astype(BF)
        out_ref[2, t * 32 : t * 32 + 16] = mm(s5, cols(ref, 10 + j5)).astype(BF)
        out_ref[2, t * 32 + 16 : t * 32 + 32] = xy_ref[x * 4 + (y ^ 1), 32 + t * 16 : 48 + t * 16]
    want = xy_col(x, y, iota((128, 256), 0))
    perm = onehot(want == iota((128, 256), 1))
    out_ref[3] = mm(perm, xy_ref[:, 0:32].reshape(256, D)).astype(BF)


def to_r_kernel(ids, q_ref, k_ref, v_ref, u_ref, g3_ref, qr_ref, own_ref, t1_ref, t2_ref, t3_ref, tmp):
    _, _, q, r = xyqr(ids[0])
    j3 = q & 1
    h1 = 3 - (r & 1)
    s3 = pick(3, j3)
    for t, ref in enumerate((q_ref, k_ref, v_ref, u_ref)):
        lo = t * 128
        tmp[0, lo : lo + 128] = ref[:, 4 * D : 5 * D]
        tmp[1, lo : lo + 128] = ref[:, 5 * D : 6 * D]
        tmp[2, lo : lo + 64] = mm(s3, cols(ref, 6 + j3)).astype(BF)
        tmp[2, lo + 64 : lo + 128] = g3_ref[t * 64 : (t + 1) * 64]
        for u in range(4):
            tmp[3, lo + u * 32 : lo + u * 32 + 32] = qr_ref[u, t * 32 : (t + 1) * 32]
        t1_ref[512 + lo : 640 + lo] = cols(ref, h1)
    for v, ref in enumerate((own_ref, t1_ref, t2_ref, t3_ref)):
        ref[0:512] = tmp[r ^ v]


def attention(qs, ks, vs, us, docs, mult):
    nb = len(qs)
    keys, vals = jnp.concatenate(ks, 0), jnp.concatenate(vs, 0)
    doc_all = jnp.concatenate(docs, 0)
    outs, dqs, dk, dv, term = [], [], None, None, jnp.zeros((1, 1), F32)
    for b in range(nb):
        raw = mm_nt(qs[b], keys)
        allowed = mm_nt(docs[b], doc_all) > 0.5
        scores = jnp.where(allowed, raw * mult, -1e30)
        expo = jnp.exp(scores - jnp.max(scores, axis=1, keepdims=True))
        probs = expo * (1.0 / jnp.sum(expo, axis=1, keepdims=True))
        low = probs.astype(BF)
        att = mm(low, vals)
        delta = jnp.sum(us[b].astype(F32) * att, axis=1, keepdims=True)
        ds = probs * (mm_nt(us[b], vals) - delta)
        term += jnp.sum(jnp.sum(ds * raw, axis=1, keepdims=True), axis=0, keepdims=True)
        ds_low = ds.astype(BF)
        outs.append(att.astype(BF))
        dqs.append((mm(ds_low, keys) * mult).astype(BF))
        dk_b, dv_b = mm_tn(ds_low, qs[b]), mm_tn(low, us[b])
        dk, dv = (dk_b, dv_b) if dk is None else (dk + dk_b, dv + dv_b)
    dk = (dk * mult).astype(BF)
    dv = dv.astype(BF)
    part = lambda z: [z[b * 128 : (b + 1) * 128] for b in range(nb)]
    return outs, dqs, part(dk), part(dv), term * (1.0 / math.sqrt(D))


def doc_bounds(sizes):
    lane = iota((1, 128), 1)
    first, end = jnp.zeros((1, 128), jnp.int32), jnp.zeros((1, 128), jnp.int32)
    at = jnp.int32(0)
    for c in range(8):
        nxt = at + sizes[c] if c < 7 else jnp.int32(1 << 30)
        first, end = jnp.where(lane == c, at, first), jnp.where(lane == c, nxt, end)
        at = nxt
    return first, end


def doc_onehot(pos, bounds):
    return onehot((pos >= bounds[0]) & (pos < bounds[1]))


def at_lane(term, head):
    return jnp.where(iota((1, 128), 1) == head, term, 0.0)


def local_kernel(ids, sharp, sizes, q_ref, k_ref, v_ref, u_ref, z0_ref, terms_ref):
    here = doc_onehot(ids[0] * 128 + iota((128, 128), 0), doc_bounds(sizes))
    total = jnp.zeros((1, 128), F32)
    for h in range(2):
        blocks = [[ref[:, h * D : (h + 1) * D]] for ref in (q_ref, k_ref, v_ref, u_ref)]
        *res, term = attention(*blocks, [here], sharp[h] * (1.0 / math.sqrt(D)))
        for t in range(4):
            z0_ref[t * 128 : (t + 1) * 128, h * D : (h + 1) * D] = res[t][0]
        total += at_lane(term, h)
    terms_ref[...] = jnp.broadcast_to(total, (8, 128))


def near_kernel(ids, sharp, sizes, q_ref, k_ref, v_ref, u_ref, g1_ref, before_ref, own_ref, back_ref, terms_ref):
    dev = ids[0]
    _, _, _, r = xyqr(dev)
    row = iota((128, 128), 0)
    bounds = doc_bounds(sizes)
    here = doc_onehot(dev * 128 + row, bounds)
    there = doc_onehot((dev ^ 1) * 128 + row, bounds)
    refs = (q_ref, k_ref, v_ref, u_ref)
    h = 2 + (r & 1)
    blocks = [[cols(ref, h), g1_ref[512 + t * 128 : 640 + t * 128]] for t, ref in enumerate(refs)]
    *res, term = attention(*blocks, [here, there], sharp[h] * (1.0 / math.sqrt(D)))
    for t in range(4):
        own_ref[t * 128 : (t + 1) * 128] = res[t][0]
        back_ref[t * 128 : (t + 1) * 128] = res[t][1]
    terms_ref[...] = before_ref[...] + jnp.broadcast_to(at_lane(term, h), (8, 128))


def pieces(v):
    hi = v.astype(BF).astype(F32)
    mid = (v - hi).astype(BF).astype(F32)
    lo = v - hi - mid
    row = iota((16, 128), 0)
    return jnp.where(row == 0, hi, jnp.where(row == 1, mid, jnp.where(row == 2, lo, 0.0))).astype(BF)


def task_kernel(ids, sharp, sizes, i0, i1, i2, i3, terms_ref, back_ref, o0, o1, o2, o3):
    ins, outs = (i0, i1, i2, i3), (o0, o1, o2, o3)
    x, y, q, r = xyqr(ids[0])
    m = iota((128, 128), 0)
    near, r3 = r < 2, r == 2
    far = r == 3
    q3 = q == 3
    u_m = jnp.where(near, q, jnp.where(r3, q ^ (m >> 6), m >> 5))
    y_m = jnp.where(far & (q == 2), y ^ ((m >> 4) & 1), jnp.where(far & q3, jnp.where(y < 2, (m >> 3) & 3, (m >> 2) & 3), y))
    x_m = jnp.where(far & q3 & (y >= 2), (m >> 4) & 1, x)
    level = jnp.where(near, 2, jnp.where(r3, 3, jnp.where(q < 2, 4, jnp.where(q == 2, 5, jnp.where(y < 2, 6, 7)))))
    j = jnp.where(near, r, jnp.where(r3, q & 1, jnp.where(q < 2, q, jnp.where(q == 2, y & 1, jnp.where(y < 2, y, x)))))
    sh = level - 2
    dil = jnp.left_shift(1, sh)
    offset = (5 + j * (dil >> 1)) & (dil - 1)
    i_m = m & (jnp.right_shift(128, sh) - 1)
    low = (x_m * 64 + y_m * 16 + u_m * 4) * 128 + i_m * dil + offset
    bounds = doc_bounds(sizes)
    docs = [doc_onehot(low + (r ^ v) * 128, bounds) for v in range(4)]
    head = level * 2 + j
    blocks = [[ref[t * 128 : (t + 1) * 128] for ref in ins] for t in range(4)]
    *res, term = attention(*blocks, docs, sharp[head] * (1.0 / math.sqrt(D)))
    extra = pieces(terms_ref[0:1] + at_lane(term, head))
    for v, ref in enumerate(outs):
        for t in range(4):
            ref[t * 128 : (t + 1) * 128] = res[t][v]
        ref[512:528] = extra
    o1[528:1040] = back_ref[...]


def total4(blocks):
    a, b, c, d = [jnp.sum(z.astype(F32), axis=0, keepdims=True) for z in blocks]
    return (a + b) + (c + d)


def from_r_kernel(ids, i0, i1, i2, i3, g3_ref, out_ref):
    _, _, _, r = xyqr(ids[0])
    ins = (i0, i1, i2, i3)
    for v, ref in enumerate(ins):

        @pl.when((r ^ v) == 2)
        def _():
            for t in range(4):
                g3_ref[t * 64 : (t + 1) * 64] = ref[t * 128 + 64 : t * 128 + 128]

        @pl.when((r ^ v) == 3)
        def _():
            for t in range(4):
                for u in range(4):
                    out_ref[u, t * 32 : (t + 1) * 32] = ref[t * 128 + u * 32 : t * 128 + u * 32 + 32]

    extra = pieces(total4([ref[512:528] for ref in ins]))
    for u in range(4):
        out_ref[u, 128:144] = extra


def from_q_kernel(ids, in_ref, g5_ref, out_ref):
    x, y, _, _ = xyqr(ids[0])
    dp = ids[1]
    want = xy_col(x, y, iota((256, 128), 1))
    perm = onehot(want == iota((256, 128), 0))
    extra = pieces(total4([in_ref[u, 128:144] for u in range(4)]))
    for d in range(32):
        out_ref[d, 0:32] = jnp.zeros((32, D), BF)
        out_ref[d, 32:48] = extra
    for t in range(4):
        g5_ref[t * 16 : (t + 1) * 16] = in_ref[2, t * 32 + 16 : t * 32 + 32]
    rows = mm(perm, in_ref[3, 0:128]).astype(BF)
    for d in range(8):
        out_ref[d * 4 + dp, 0:32] = rows[d * 32 : (d + 1) * 32]


def spread(level, j):
    n = 128 // DIL[level]
    return onehot(iota((128, n), 0) == iota((128, n), 1) * DIL[level] + off(level, j))


def put(ref, head, value):
    ref[:, pl.ds(pl.multiple_of(head * D, D), D)] = value.astype(BF)


def unpack_low_kernel(ids, z0_ref, own_ref, r0, r1, r2, r3, o_ref, dq_ref, dk_ref, dv_ref, mine_ref):
    _, _, q, r = xyqr(ids[0])
    res = (o_ref, dq_ref, dk_ref, dv_ref)
    j1, j3 = r & 1, q & 1
    for t, ref in enumerate(res):
        lo = t * 128
        ref[:, : 2 * D] = z0_ref[lo : lo + 128]
        put(ref, 2 + j1, own_ref[lo : lo + 128])
        put(ref, 3 - j1, r1[528 + lo : 656 + lo])
    for v, src in enumerate((r0, r1, r2, r3)):
        role = r ^ v

        @pl.when(role < 2)
        def _():
            for t, ref in enumerate(res):
                put(ref, 4 + role, src[t * 128 : (t + 1) * 128])

        @pl.when(role == 2)
        def _():
            w3 = spread(3, j3)
            for t in range(4):
                mine_ref[t] = mm(w3, src[t * 128 : t * 128 + 64]).astype(BF)


def unpack_high_kernel(ids, l0, l1, l2, l3, mine_ref, g3_ref, qr_ref, g5_ref, xy_ref, o_ref, dq_ref, dk_ref, dv_ref, terms_ref):
    x, y, q, _ = xyqr(ids[0])
    dp = ids[1]
    res = (o_ref, dq_ref, dk_ref, dv_ref)
    j3, j5 = q & 1, y & 1
    w3b = spread(3, 1 - j3)
    w40, w41, w5, w5b = spread(4, 0), spread(4, 1), spread(5, j5), spread(5, 1 - j5)
    pi, ci = iota((128, 32), 0), iota((128, 32), 1)
    for t, ref in enumerate(res):
        put(ref, j3, mine_ref[t])
        put(ref, 1 - j3, mm(w3b, g3_ref[t * 64 : (t + 1) * 64]))
        put(ref, 2, mm(w40, qr_ref[0, t * 32 : (t + 1) * 32]))
        put(ref, 3, mm(w41, qr_ref[1, t * 32 : (t + 1) * 32]))
        put(ref, 4 + j5, mm(w5, qr_ref[2, t * 32 : t * 32 + 16]))
        put(ref, 5 - j5, mm(w5b, g5_ref[t * 16 : (t + 1) * 16]))
        for j in range(2):
            w6 = onehot(pi == (ci - t * 8) * 16 + off(6, j))
            w7 = onehot(pi == (ci - t * 4) * 32 + off(7, j))
            put(ref, 6 + j, mm(w6, xy_ref[(x * 4 + j) * 4 + dp, 0:32]))
            put(ref, 8 + j, mm(w7, xy_ref[(j * 4 + 2) * 4 + dp, 0:32]))
    acc = xy_ref[0, 32:48].astype(F32)
    for d in range(1, 32):
        acc += xy_ref[d, 32:48].astype(F32)
    terms_ref[...] = jnp.sum(acc, axis=0, keepdims=True)[:, :16]


SMEM = pl.BlockSpec(memory_space=pltpu.SMEM)
VMEM = pl.BlockSpec(memory_space=pltpu.VMEM)
LIMIT = pltpu.CompilerParams(vmem_limit_bytes=20 << 20)


def stay(array):
    return pltpu.with_memory_space_constraint(array, pltpu.VMEM)


def call(kernel, outs, scalars, params, rest, scratch=(), out_space=pltpu.VMEM):
    shapes = [out_space(s, d) for s, d in outs]
    single = len(shapes) == 1
    run = pl.pallas_call(
        kernel,
        in_specs=[SMEM] * len(scalars) + [VMEM] * (len(params) + len(rest)),
        out_specs=VMEM if single else [VMEM] * len(shapes),
        out_shape=shapes[0] if single else shapes,
        scratch_shapes=list(scratch),
        compiler_params=LIMIT,
    )
    args = [*params, *[stay(a) for a in rest]]
    return run(*scalars, *args)


def swap(array, axis, v):
    return lax.ppermute(array, axis, [(i, i ^ v) for i in range(4)])


def body(asking_vectors, lookup_vectors, payload_vectors, incoming_sensitivity, learned_sharpness, reply_list_sizes):
    raw = [a[0] for a in (asking_vectors, lookup_vectors, payload_vectors, incoming_sensitivity)]
    ids = jnp.stack([lax.axis_index(SEQ), lax.axis_index("dp")]).astype(jnp.int32)
    block = lambda n: ((n, D), BF)
    held = [pltpu.with_memory_space_constraint(a, pltpu.HBM) for a in raw]
    g3, xy = pl.pallas_call(
        pack_kernel,
        grid=(1,),
        in_specs=[SMEM]
        + [pl.BlockSpec((128, 2 * D), lambda i: (0, 3))] * 4
        + [pl.BlockSpec((128, 8 * D), lambda i: (0, 1))] * 4,
        out_specs=[pl.BlockSpec((256, D), lambda i: (0, 0)), pl.BlockSpec((8, 96, D), lambda i: (0, 0, 0))],
        out_shape=[jax.ShapeDtypeStruct((256, D), BF), jax.ShapeDtypeStruct((8, 96, D), BF)],
        compiler_params=LIMIT,
        name="pack",
    )(ids, *held, *held)
    g3 = swap(g3, "q", 1)
    xy = lax.all_to_all(xy, ("x", "y"), 0, 0)
    four = [stay(a) for a in raw]
    sizes = reply_list_sizes[0]
    z0, terms = call(local_kernel, [((512, 2 * D), BF), ((8, 128), F32)], [ids, learned_sharpness, sizes], four, [])
    qs = call(to_q_kernel, [((4, 128, D), BF)], [ids], four, [xy])
    qs = lax.all_to_all(qs, "q", 0, 0)
    r0, r1, r2, r3 = call(
        to_r_kernel, [block(512), block(1024), block(512), block(512)], [ids], four, [g3, qs],
        [pltpu.VMEM((4, 512, D), BF)],
    )
    r1, r3, r2 = swap(r1, "r", 1), swap(r3, "r", 3), swap(r2, "r", 2)
    own1, back1, terms = call(
        near_kernel, [block(512), block(512), ((8, 128), F32)], [ids, learned_sharpness, sizes], four, [r1, terms]
    )
    r0, r1, r2, r3 = call(
        task_kernel, [block(528), block(1040), block(528), block(528)], [ids, learned_sharpness, sizes], [],
        [r0, r1, r2, r3, terms, back1],
    )
    r3, r2, r1 = swap(r3, "r", 3), swap(r2, "r", 2), swap(r1, "r", 1)
    back3, qs = call(from_r_kernel, [block(256), ((4, 144, D), BF)], [ids], [], [r0, r1, r2, r3])
    qs = lax.all_to_all(qs, "q", 0, 0)
    back3 = swap(back3, "q", 1)
    back5, xy = call(from_q_kernel, [block(64), ((32, 48, D), BF)], [ids], [], [qs])
    xy = lax.all_to_all(xy, ("x", "y", "dp"), 0, 0)
    back5 = swap(back5, "y", 1)
    result = jax.ShapeDtypeStruct((128, 16 * D), BF)
    args = [stay(a) for a in (z0, own1, r0, r1, r2, r3)]
    *outs, mine = pl.pallas_call(
        unpack_low_kernel,
        grid=(1,),
        in_specs=[SMEM] + [VMEM] * len(args),
        out_specs=[pl.BlockSpec((128, 6 * D), lambda i: (0, 0))] * 4 + [pl.BlockSpec((4, 128, D), lambda i: (0, 0, 0))],
        out_shape=[result] * 4 + [jax.ShapeDtypeStruct((4, 128, D), BF)],
        compiler_params=LIMIT,
        name="unpack_low",
    )(ids, *args)
    args = [stay(a) for a in (mine, back3, qs, back5, xy)]
    high = pl.BlockSpec((pl.Element(128), pl.Element(10 * D)), lambda i: (0, 6 * D))
    *outs, terms = pl.pallas_call(
        unpack_high_kernel,
        grid=(1,),
        in_specs=[SMEM] + [pl.BlockSpec(memory_space=pl.ANY)] * 4 + [VMEM] * len(args),
        out_specs=[high] * 4 + [pl.BlockSpec((1, 16), lambda i: (0, 0))],
        out_shape=[result] * 4 + [jax.ShapeDtypeStruct((1, 16), F32)],
        input_output_aliases={1: 0, 2: 1, 3: 2, 4: 3},
        compiler_params=LIMIT,
        name="unpack_high",
    )(ids, *outs, *args)
    return (*[o[None] for o in outs], terms[0])


def solution(mesh):
    fine = Mesh(mesh.devices.reshape(2, 4, 4, 4, 4), SEQ + ("dp",))
    rows = P("dp", SEQ, None)
    in_specs = (rows, rows, rows, rows, P(), P("dp", None))
    out_specs = (rows, rows, rows, rows, P())
    return jax.shard_map(body, mesh=fine, in_specs=in_specs, out_specs=out_specs, check_vma=False)
```

```python
import math

import jax
import jax.numpy as jnp
from jax import lax
from jax.experimental import pallas as pl
from jax.experimental.pallas import tpu as pltpu
from jax.sharding import Mesh, PartitionSpec as P


D = 128
BF = jnp.bfloat16
F32 = jnp.float32
DIL = (1, 1, 1, 2, 4, 8, 16, 32)
SEQ = ("x", "y", "q", "r")


def off(level, j):
    dil = DIL[level]
    return (5 + j * (dil // 2)) % dil


def iota(shape, dim):
    return lax.broadcasted_iota(jnp.int32, shape, dim)


def onehot(cond):
    return cond.astype(F32).astype(BF)


def mm(a, b):
    return jnp.dot(a, b, preferred_element_type=F32)


def mm_nt(a, b):
    return lax.dot_general(a, b, (((1,), (1,)), ((), ())), preferred_element_type=F32)


def mm_tn(a, b):
    return lax.dot_general(a, b, (((0,), (0,)), ((), ())), preferred_element_type=F32)


def pick(level, j):
    n = 128 // DIL[level]
    return onehot(iota((n, 128), 1) == iota((n, 128), 0) * DIL[level] + off(level, j))


def cols(ref, head, first=0):
    return ref[:, pl.ds(pl.multiple_of((head - first) * D, D), D)]


def xyqr(dev):
    return dev >> 6, (dev >> 4) & 3, (dev >> 2) & 3, dev & 3


def xy_col(x, y, row):
    t, m = row >> 5, row & 31
    six = (x * 4 + (m >> 3)) * 32 + t * 8 + (m & 7)
    seven = (m >> 2) * 32 + t * 4 + (m & 3)
    return jnp.where(y < 2, six, jnp.where(y == 2, seven, -1))


def pack_kernel(ids, q_ref, k_ref, v_ref, u_ref, xy_ref):
    x, y, _, _ = xyqr(ids[0])
    srcs = (q_ref, k_ref, v_ref, u_ref)
    j5 = 1 - (y & 1)
    s5 = pick(5, j5)
    xy_ref[...] = jnp.zeros(xy_ref.shape, BF)
    for t, ref in enumerate(srcs):
        xy_ref[x * 4 + (y ^ 1), 32 + t * 16 : 48 + t * 16] = mm(s5, cols(ref, 2 + j5)).astype(BF)
    for j in range(2):
        acc6 = jnp.zeros((32, D), F32)
        acc7 = jnp.zeros((32, D), F32)
        ri, ci = iota((32, 128), 0), iota((32, 128), 1)
        for t, ref in enumerate(srcs):
            w6 = onehot((ci == (ri - t * 8) * 16 + off(6, j)))
            w7 = onehot((ci == (ri - t * 4) * 32 + off(7, j)))
            acc6 += mm(w6, ref[:, (4 + j) * D : (5 + j) * D])
            acc7 += mm(w7, ref[:, (6 + j) * D : (7 + j) * D])
        xy_ref[x * 4 + j, 0:32] = acc6.astype(BF)
        xy_ref[j * 4 + 2, 0:32] = acc7.astype(BF)


def to_q_kernel(ids, q_ref, k_ref, v_ref, u_ref, xy_ref, out_ref):
    x, y, _, _ = xyqr(ids[0])
    j5 = y & 1
    s40, s41, s5 = pick(4, 0), pick(4, 1), pick(5, j5)
    for t, ref in enumerate((q_ref, k_ref, v_ref, u_ref)):
        out_ref[0, t * 32 : (t + 1) * 32] = mm(s40, ref[:, 8 * D : 9 * D]).astype(BF)
        out_ref[1, t * 32 : (t + 1) * 32] = mm(s41, ref[:, 9 * D : 10 * D]).astype(BF)
        out_ref[2, t * 32 : t * 32 + 16] = mm(s5, cols(ref, 10 + j5)).astype(BF)
        out_ref[2, t * 32 + 16 : t * 32 + 32] = xy_ref[x * 4 + (y ^ 1), 32 + t * 16 : 48 + t * 16]
    want = xy_col(x, y, iota((128, 256), 0))
    perm = onehot(want == iota((128, 256), 1))
    out_ref[3] = mm(perm, xy_ref[:, 0:32].reshape(256, D)).astype(BF)


def early_kernel(ids, q_ref, k_ref, v_ref, u_ref, g3_ref, own_ref, e1_ref, e2_ref, e3_ref):
    _, _, q, r = xyqr(ids[0])
    j3 = 1 - (q & 1)
    h1 = 3 - (r & 1)
    s3 = pick(3, j3)
    for t, ref in enumerate((q_ref, k_ref, v_ref, u_ref)):
        lo = t * 128
        g3_ref[t * 64 : (t + 1) * 64] = mm(s3, cols(ref, 6 + j3)).astype(BF)
        for v, out in enumerate((own_ref, e1_ref, e2_ref, e3_ref)):
            out[lo : lo + 128] = cols(ref, 4 + ((r ^ v) & 1))
        e1_ref[512 + lo : 640 + lo] = cols(ref, h1)


def to_r_kernel(ids, q_ref, k_ref, v_ref, u_ref, g3_ref, qr_ref, own_ref, t1_ref, t2_ref, t3_ref, tmp):
    _, _, q, r = xyqr(ids[0])
    j3 = q & 1
    s3 = pick(3, j3)
    for t, ref in enumerate((q_ref, k_ref, v_ref, u_ref)):
        lo = t * 128
        tmp[0, lo : lo + 64] = mm(s3, cols(ref, 6 + j3)).astype(BF)
        tmp[0, lo + 64 : lo + 128] = g3_ref[t * 64 : (t + 1) * 64]
        for u in range(4):
            tmp[1, lo + u * 32 : lo + u * 32 + 32] = qr_ref[u, t * 32 : (t + 1) * 32]
    for v, ref in enumerate((own_ref, t1_ref, t2_ref, t3_ref)):
        ref[...] = tmp[(r ^ v) & 1]


def attention(qs, ks, vs, us, docs, mult):
    nb = len(qs)
    keys, vals = jnp.concatenate(ks, 0), jnp.concatenate(vs, 0)
    doc_all = jnp.concatenate(docs, 0)
    outs, dqs, dk, dv, term = [], [], None, None, jnp.zeros((1, 1), F32)
    for b in range(nb):
        raw = mm_nt(qs[b], keys)
        allowed = mm_nt(docs[b], doc_all) > 0.5
        scores = jnp.where(allowed, raw * mult, -1e30)
        expo = jnp.exp(scores - jnp.max(scores, axis=1, keepdims=True))
        probs = expo * (1.0 / jnp.sum(expo, axis=1, keepdims=True))
        low = probs.astype(BF)
        att = mm(low, vals)
        delta = jnp.sum(us[b].astype(F32) * att, axis=1, keepdims=True)
        ds = probs * (mm_nt(us[b], vals) - delta)
        term += jnp.sum(jnp.sum(ds * raw, axis=1, keepdims=True), axis=0, keepdims=True)
        ds_low = ds.astype(BF)
        outs.append(att.astype(BF))
        dqs.append((mm(ds_low, keys) * mult).astype(BF))
        dk_b, dv_b = mm_tn(ds_low, qs[b]), mm_tn(low, us[b])
        dk, dv = (dk_b, dv_b) if dk is None else (dk + dk_b, dv + dv_b)
    dk = (dk * mult).astype(BF)
    dv = dv.astype(BF)
    part = lambda z: [z[b * 128 : (b + 1) * 128] for b in range(nb)]
    return outs, dqs, part(dk), part(dv), term * (1.0 / math.sqrt(D))


def doc_bounds(sizes):
    lane = iota((1, 128), 1)
    first, end = jnp.zeros((1, 128), jnp.int32), jnp.zeros((1, 128), jnp.int32)
    at = jnp.int32(0)
    for c in range(8):
        nxt = at + sizes[c] if c < 7 else jnp.int32(1 << 30)
        first, end = jnp.where(lane == c, at, first), jnp.where(lane == c, nxt, end)
        at = nxt
    return first, end


def doc_onehot(pos, bounds):
    return onehot((pos >= bounds[0]) & (pos < bounds[1]))


def at_lane(term, head):
    return jnp.where(iota((1, 128), 1) == head, term, 0.0)


def local_kernel(ids, sharp, sizes, q_ref, k_ref, v_ref, u_ref, z0_ref, terms_ref):
    here = doc_onehot(ids[0] * 128 + iota((128, 128), 0), doc_bounds(sizes))
    total = jnp.zeros((1, 128), F32)
    for h in range(2):
        blocks = [[ref[:, h * D : (h + 1) * D]] for ref in (q_ref, k_ref, v_ref, u_ref)]
        *res, term = attention(*blocks, [here], sharp[h] * (1.0 / math.sqrt(D)))
        for t in range(4):
            z0_ref[t * 128 : (t + 1) * 128, h * D : (h + 1) * D] = res[t][0]
        total += at_lane(term, h)
    terms_ref[...] = jnp.broadcast_to(total, (8, 128))


def near_kernel(ids, sharp, sizes, q_ref, k_ref, v_ref, u_ref, g1_ref, before_ref, own_ref, back_ref, terms_ref):
    dev = ids[0]
    _, _, _, r = xyqr(dev)
    row = iota((128, 128), 0)
    bounds = doc_bounds(sizes)
    here = doc_onehot(dev * 128 + row, bounds)
    there = doc_onehot((dev ^ 1) * 128 + row, bounds)
    refs = (q_ref, k_ref, v_ref, u_ref)
    h = 2 + (r & 1)
    blocks = [[cols(ref, h), g1_ref[512 + t * 128 : 640 + t * 128]] for t, ref in enumerate(refs)]
    *res, term = attention(*blocks, [here, there], sharp[h] * (1.0 / math.sqrt(D)))
    for t in range(4):
        own_ref[t * 128 : (t + 1) * 128] = res[t][0]
        back_ref[t * 128 : (t + 1) * 128] = res[t][1]
    terms_ref[...] = before_ref[...] + jnp.broadcast_to(at_lane(term, h), (8, 128))


def pieces(v):
    hi = v.astype(BF).astype(F32)
    mid = (v - hi).astype(BF).astype(F32)
    lo = v - hi - mid
    row = iota((16, 128), 0)
    return jnp.where(row == 0, hi, jnp.where(row == 1, mid, jnp.where(row == 2, lo, 0.0))).astype(BF)


def task_kernel(ids, sharp, sizes, e0, e1, e2, e3, i0, i1, i2, i3, terms_ref, back_ref, o0, o1, o2, o3):
    ins, outs = ((e0, i0), (e1, i1), (e2, i2), (e3, i3)), (o0, o1, o2, o3)
    x, y, q, r = xyqr(ids[0])
    m = iota((128, 128), 0)
    near, r3 = r < 2, r == 2
    far = r == 3
    q3 = q == 3
    u_m = jnp.where(near, q, jnp.where(r3, q ^ (m >> 6), m >> 5))
    y_m = jnp.where(far & (q == 2), y ^ ((m >> 4) & 1), jnp.where(far & q3, jnp.where(y < 2, (m >> 3) & 3, (m >> 2) & 3), y))
    x_m = jnp.where(far & q3 & (y >= 2), (m >> 4) & 1, x)
    level = jnp.where(near, 2, jnp.where(r3, 3, jnp.where(q < 2, 4, jnp.where(q == 2, 5, jnp.where(y < 2, 6, 7)))))
    j = jnp.where(near, r, jnp.where(r3, q & 1, jnp.where(q < 2, q, jnp.where(q == 2, y & 1, jnp.where(y < 2, y, x)))))
    sh = level - 2
    dil = jnp.left_shift(1, sh)
    offset = (5 + j * (dil >> 1)) & (dil - 1)
    i_m = m & (jnp.right_shift(128, sh) - 1)
    low = (x_m * 64 + y_m * 16 + u_m * 4) * 128 + i_m * dil + offset
    bounds = doc_bounds(sizes)
    docs = [doc_onehot(low + (r ^ v) * 128, bounds) for v in range(4)]
    head = level * 2 + j
    at = lambda ref, t: ref[t * 128 : (t + 1) * 128]
    blocks = [[jnp.where(r < 2, at(a, t), at(b, t)) for a, b in ins] for t in range(4)]
    *res, term = attention(*blocks, docs, sharp[head] * (1.0 / math.sqrt(D)))
    extra = pieces(terms_ref[0:1] + at_lane(term, head))
    for v, ref in enumerate(outs):
        for t in range(4):
            ref[t * 128 : (t + 1) * 128] = res[t][v]
        ref[512:528] = extra
    o1[528:1040] = back_ref[...]


def total4(blocks):
    a, b, c, d = [jnp.sum(z.astype(F32), axis=0, keepdims=True) for z in blocks]
    return (a + b) + (c + d)


def from_r_kernel(ids, i0, i1, i2, i3, g3_ref, out_ref):
    _, _, _, r = xyqr(ids[0])
    ins = (i0, i1, i2, i3)
    for v, ref in enumerate(ins):

        @pl.when((r ^ v) == 2)
        def _():
            for t in range(4):
                g3_ref[t * 64 : (t + 1) * 64] = ref[t * 128 + 64 : t * 128 + 128]

        @pl.when((r ^ v) == 3)
        def _():
            for t in range(4):
                for u in range(4):
                    out_ref[u, t * 32 : (t + 1) * 32] = ref[t * 128 + u * 32 : t * 128 + u * 32 + 32]

    extra = pieces(total4([ref[512:528] for ref in ins]))
    for u in range(4):
        out_ref[u, 128:144] = extra


def from_q_kernel(ids, in_ref, g5_ref, out_ref):
    x, y, _, _ = xyqr(ids[0])
    dp = ids[1]
    want = xy_col(x, y, iota((256, 128), 1))
    perm = onehot(want == iota((256, 128), 0))
    extra = pieces(total4([in_ref[u, 128:144] for u in range(4)]))
    for d in range(32):
        out_ref[d, 0:32] = jnp.zeros((32, D), BF)
        out_ref[d, 32:48] = extra
    for t in range(4):
        g5_ref[t * 16 : (t + 1) * 16] = in_ref[2, t * 32 + 16 : t * 32 + 32]
    rows = mm(perm, in_ref[3, 0:128]).astype(BF)
    for d in range(8):
        out_ref[d * 4 + dp, 0:32] = rows[d * 32 : (d + 1) * 32]


def spread(level, j):
    n = 128 // DIL[level]
    return onehot(iota((128, n), 0) == iota((128, n), 1) * DIL[level] + off(level, j))


def put(ref, head, value):
    ref[:, pl.ds(pl.multiple_of(head * D, D), D)] = value.astype(BF)


def unpack_low_kernel(ids, z0_ref, own_ref, r0, r1, r2, r3, o_ref, dq_ref, dk_ref, dv_ref, mine_ref):
    _, _, q, r = xyqr(ids[0])
    res = (o_ref, dq_ref, dk_ref, dv_ref)
    j1, j3 = r & 1, q & 1
    for t, ref in enumerate(res):
        lo = t * 128
        ref[:, : 2 * D] = z0_ref[lo : lo + 128]
        put(ref, 2 + j1, own_ref[lo : lo + 128])
        put(ref, 3 - j1, r1[528 + lo : 656 + lo])
    for v, src in enumerate((r0, r1, r2, r3)):
        role = r ^ v

        @pl.when(role < 2)
        def _():
            for t, ref in enumerate(res):
                put(ref, 4 + role, src[t * 128 : (t + 1) * 128])

        @pl.when(role == 2)
        def _():
            w3 = spread(3, j3)
            for t in range(4):
                mine_ref[t] = mm(w3, src[t * 128 : t * 128 + 64]).astype(BF)


def unpack_high_kernel(ids, l0, l1, l2, l3, mine_ref, g3_ref, qr_ref, g5_ref, xy_ref, o_ref, dq_ref, dk_ref, dv_ref, terms_ref):
    x, y, q, _ = xyqr(ids[0])
    dp = ids[1]
    res = (o_ref, dq_ref, dk_ref, dv_ref)
    j3, j5 = q & 1, y & 1
    w3b = spread(3, 1 - j3)
    w40, w41, w5, w5b = spread(4, 0), spread(4, 1), spread(5, j5), spread(5, 1 - j5)
    pi, ci = iota((128, 32), 0), iota((128, 32), 1)
    for t, ref in enumerate(res):
        put(ref, j3, mine_ref[t])
        put(ref, 1 - j3, mm(w3b, g3_ref[t * 64 : (t + 1) * 64]))
        put(ref, 2, mm(w40, qr_ref[0, t * 32 : (t + 1) * 32]))
        put(ref, 3, mm(w41, qr_ref[1, t * 32 : (t + 1) * 32]))
        put(ref, 4 + j5, mm(w5, qr_ref[2, t * 32 : t * 32 + 16]))
        put(ref, 5 - j5, mm(w5b, g5_ref[t * 16 : (t + 1) * 16]))
        for j in range(2):
            w6 = onehot(pi == (ci - t * 8) * 16 + off(6, j))
            w7 = onehot(pi == (ci - t * 4) * 32 + off(7, j))
            put(ref, 6 + j, mm(w6, xy_ref[(x * 4 + j) * 4 + dp, 0:32]))
            put(ref, 8 + j, mm(w7, xy_ref[(j * 4 + 2) * 4 + dp, 0:32]))
    acc = xy_ref[0, 32:48].astype(F32)
    for d in range(1, 32):
        acc += xy_ref[d, 32:48].astype(F32)
    terms_ref[...] = jnp.sum(acc, axis=0, keepdims=True)[:, :16]


SMEM = pl.BlockSpec(memory_space=pltpu.SMEM)
VMEM = pl.BlockSpec(memory_space=pltpu.VMEM)
LIMIT = pltpu.CompilerParams(vmem_limit_bytes=12 << 20)


def stay(array):
    return pltpu.with_memory_space_constraint(array, pltpu.VMEM)


def call(kernel, outs, scalars, params, rest, scratch=(), out_space=pltpu.VMEM):
    shapes = [out_space(s, d) for s, d in outs]
    single = len(shapes) == 1
    run = pl.pallas_call(
        kernel,
        in_specs=[SMEM] * len(scalars) + [VMEM] * (len(params) + len(rest)),
        out_specs=VMEM if single else [VMEM] * len(shapes),
        out_shape=shapes[0] if single else shapes,
        scratch_shapes=list(scratch),
        compiler_params=LIMIT,
    )
    args = [*params, *[stay(a) for a in rest]]
    return run(*scalars, *args)


def swap(array, axis, v):
    return lax.ppermute(array, axis, [(i, i ^ v) for i in range(4)])


def send(array, v, senders):
    return lax.ppermute(array, "r", [(i, i ^ v) for i in senders])


def body(asking_vectors, lookup_vectors, payload_vectors, incoming_sensitivity, learned_sharpness, reply_list_sizes):
    raw = [a[0] for a in (asking_vectors, lookup_vectors, payload_vectors, incoming_sensitivity)]
    ids = jnp.stack([lax.axis_index(SEQ), lax.axis_index("dp")]).astype(jnp.int32)
    block = lambda n: ((n, D), BF)
    held = [pltpu.with_memory_space_constraint(a, pltpu.HBM) for a in raw]
    xy = pl.pallas_call(
        pack_kernel,
        grid=(1,),
        in_specs=[SMEM] + [pl.BlockSpec((128, 8 * D), lambda i: (0, 1))] * 4,
        out_specs=pl.BlockSpec((8, 96, D), lambda i: (0, 0, 0)),
        out_shape=jax.ShapeDtypeStruct((8, 96, D), BF),
        compiler_params=LIMIT,
        name="pack",
    )(ids, *held)
    xy = lax.all_to_all(xy, ("x", "y"), 0, 0)
    four = [stay(a) for a in raw]
    sizes = reply_list_sizes[0]
    z0, terms = call(local_kernel, [((512, 2 * D), BF), ((8, 128), F32)], [ids, learned_sharpness, sizes], four, [])
    g3, e0, e1, e2, e3 = call(
        early_kernel, [block(256), block(512), block(1024), block(512), block(512)], [ids], four, []
    )
    qs = call(to_q_kernel, [((4, 128, D), BF)], [ids], four, [xy])
    qs = lax.all_to_all(qs, "q", 0, 0)
    g3 = swap(g3, "q", 1)
    e1, e2, e3 = swap(e1, "r", 1), send(e2, 2, (2, 3)), send(e3, 3, (2, 3))
    r0, r1, r2, r3 = call(to_r_kernel, [block(512)] * 4, [ids], four, [g3, qs], [pltpu.VMEM((2, 512, D), BF)])
    r2, r3, r1 = send(r2, 2, (0, 1)), send(r3, 3, (0, 1)), send(r1, 1, (2, 3))
    own1, back1, terms = call(
        near_kernel, [block(512), block(512), ((8, 128), F32)], [ids, learned_sharpness, sizes], four, [e1, terms]
    )
    r0, r1, r2, r3 = call(
        task_kernel, [block(528), block(1040), block(528), block(528)], [ids, learned_sharpness, sizes], [],
        [e0, e1, e2, e3, r0, r1, r2, r3, terms, back1],
    )
    r3, r2, r1 = swap(r3, "r", 3), swap(r2, "r", 2), swap(r1, "r", 1)
    back3, qs = call(from_r_kernel, [block(256), ((4, 144, D), BF)], [ids], [], [r0, r1, r2, r3])
    qs = lax.all_to_all(qs, "q", 0, 0)
    back3 = swap(back3, "q", 1)
    back5, xy = call(from_q_kernel, [block(64), ((32, 48, D), BF)], [ids], [], [qs])
    xy = lax.all_to_all(xy, ("x", "y", "dp"), 0, 0)
    back5 = swap(back5, "y", 1)
    result = jax.ShapeDtypeStruct((128, 16 * D), BF)
    args = [stay(a) for a in (z0, own1, r0, r1, r2, r3)]
    *outs, mine = pl.pallas_call(
        unpack_low_kernel,
        grid=(1,),
        in_specs=[SMEM] + [VMEM] * len(args),
        out_specs=[pl.BlockSpec((128, 6 * D), lambda i: (0, 0))] * 4 + [pl.BlockSpec((4, 128, D), lambda i: (0, 0, 0))],
        out_shape=[result] * 4 + [jax.ShapeDtypeStruct((4, 128, D), BF)],
        compiler_params=LIMIT,
        name="unpack_low",
    )(ids, *args)
    args = [stay(a) for a in (mine, back3, qs, back5, xy)]
    high = pl.BlockSpec((pl.Element(128), pl.Element(10 * D)), lambda i: (0, 6 * D))
    *outs, terms = pl.pallas_call(
        unpack_high_kernel,
        grid=(1,),
        in_specs=[SMEM] + [pl.BlockSpec(memory_space=pl.ANY)] * 4 + [VMEM] * len(args),
        out_specs=[high] * 4 + [pl.BlockSpec((1, 16), lambda i: (0, 0))],
        out_shape=[result] * 4 + [jax.ShapeDtypeStruct((1, 16), F32)],
        input_output_aliases={1: 0, 2: 1, 3: 2, 4: 3},
        compiler_params=LIMIT,
        name="unpack_high",
    )(ids, *outs, *args)
    return (*[o[None] for o in outs], terms[0])


def solution(mesh):
    fine = Mesh(mesh.devices.reshape(2, 4, 4, 4, 4), SEQ + ("dp",))
    rows = P("dp", SEQ, None)
    in_specs = (rows, rows, rows, rows, P(), P("dp", None))
    out_specs = (rows, rows, rows, rows, P())
    return jax.shard_map(body, mesh=fine, in_specs=in_specs, out_specs=out_specs, check_vma=False)
```

```python
import math

import jax
import jax.numpy as jnp
from jax import lax
from jax.experimental import pallas as pl
from jax.experimental.pallas import tpu as pltpu
from jax.sharding import Mesh, PartitionSpec as P


D = 128
BF = jnp.bfloat16
F32 = jnp.float32
DIL = (1, 1, 1, 2, 4, 8, 16, 32)
SEQ = ("x", "y", "q", "r")


def off(level, j):
    dil = DIL[level]
    return (5 + j * (dil // 2)) % dil


def iota(shape, dim):
    return lax.broadcasted_iota(jnp.int32, shape, dim)


def onehot(cond):
    return cond.astype(F32).astype(BF)


def mm(a, b):
    return jnp.dot(a, b, preferred_element_type=F32)


def mm_nt(a, b):
    return lax.dot_general(a, b, (((1,), (1,)), ((), ())), preferred_element_type=F32)


def mm_tn(a, b):
    return lax.dot_general(a, b, (((0,), (0,)), ((), ())), preferred_element_type=F32)


def pick(level, j):
    n = 128 // DIL[level]
    return onehot(iota((n, 128), 1) == iota((n, 128), 0) * DIL[level] + off(level, j))


def cols(ref, head, first=0):
    return ref[:, pl.ds(pl.multiple_of((head - first) * D, D), D)]


def xyqr(dev):
    return dev >> 6, (dev >> 4) & 3, (dev >> 2) & 3, dev & 3


def xy_col(x, y, row):
    t, m = row >> 5, row & 31
    six = (x * 4 + (m >> 3)) * 32 + t * 8 + (m & 7)
    seven = (m >> 2) * 32 + t * 4 + (m & 3)
    return jnp.where(y < 2, six, jnp.where(y == 2, seven, -1))


def pack_kernel(ids, q_ref, k_ref, v_ref, u_ref, xy_ref):
    x, y, _, _ = xyqr(ids[0])
    srcs = (q_ref, k_ref, v_ref, u_ref)
    j5 = 1 - (y & 1)
    s5 = pick(5, j5)
    xy_ref[...] = jnp.zeros(xy_ref.shape, BF)
    for t, ref in enumerate(srcs):
        xy_ref[x * 4 + (y ^ 1), 32 + t * 16 : 48 + t * 16] = mm(s5, cols(ref, 2 + j5)).astype(BF)
    for j in range(2):
        acc6 = jnp.zeros((32, D), F32)
        acc7 = jnp.zeros((32, D), F32)
        ri, ci = iota((32, 128), 0), iota((32, 128), 1)
        for t, ref in enumerate(srcs):
            w6 = onehot((ci == (ri - t * 8) * 16 + off(6, j)))
            w7 = onehot((ci == (ri - t * 4) * 32 + off(7, j)))
            acc6 += mm(w6, ref[:, (4 + j) * D : (5 + j) * D])
            acc7 += mm(w7, ref[:, (6 + j) * D : (7 + j) * D])
        xy_ref[x * 4 + j, 0:32] = acc6.astype(BF)
        xy_ref[j * 4 + 2, 0:32] = acc7.astype(BF)


def to_q_kernel(ids, q_ref, k_ref, v_ref, u_ref, xy_ref, out_ref):
    x, y, _, _ = xyqr(ids[0])
    j5 = y & 1
    s40, s41, s5 = pick(4, 0), pick(4, 1), pick(5, j5)
    for t, ref in enumerate((q_ref, k_ref, v_ref, u_ref)):
        out_ref[0, t * 32 : (t + 1) * 32] = mm(s40, ref[:, 8 * D : 9 * D]).astype(BF)
        out_ref[1, t * 32 : (t + 1) * 32] = mm(s41, ref[:, 9 * D : 10 * D]).astype(BF)
        out_ref[2, t * 32 : t * 32 + 16] = mm(s5, cols(ref, 10 + j5)).astype(BF)
        out_ref[2, t * 32 + 16 : t * 32 + 32] = xy_ref[x * 4 + (y ^ 1), 32 + t * 16 : 48 + t * 16]
    want = xy_col(x, y, iota((128, 256), 0))
    perm = onehot(want == iota((128, 256), 1))
    out_ref[3] = mm(perm, xy_ref[:, 0:32].reshape(256, D)).astype(BF)


def early_kernel(ids, q_ref, k_ref, v_ref, u_ref, g1_ref, g3_ref):
    _, _, q, r = xyqr(ids[0])
    j3 = 1 - (q & 1)
    h1 = 3 - (r & 1)
    s3 = pick(3, j3)
    for t, ref in enumerate((q_ref, k_ref, v_ref, u_ref)):
        g1_ref[t * 128 : (t + 1) * 128] = cols(ref, h1)
        g3_ref[t * 64 : (t + 1) * 64] = mm(s3, cols(ref, 6 + j3)).astype(BF)


def to_r_kernel(ids, q_ref, k_ref, v_ref, u_ref, g3_ref, qr_ref, own_ref, t1_ref, t2_ref, t3_ref, tmp):
    _, _, q, r = xyqr(ids[0])
    j3 = q & 1
    s3 = pick(3, j3)
    for t, ref in enumerate((q_ref, k_ref, v_ref, u_ref)):
        lo = t * 128
        tmp[0, lo : lo + 128] = ref[:, 4 * D : 5 * D]
        tmp[1, lo : lo + 128] = ref[:, 5 * D : 6 * D]
        tmp[2, lo : lo + 64] = mm(s3, cols(ref, 6 + j3)).astype(BF)
        tmp[2, lo + 64 : lo + 128] = g3_ref[t * 64 : (t + 1) * 64]
        for u in range(4):
            tmp[3, lo + u * 32 : lo + u * 32 + 32] = qr_ref[u, t * 32 : (t + 1) * 32]
    for v, ref in enumerate((own_ref, t1_ref, t2_ref, t3_ref)):
        ref[...] = tmp[r ^ v]


def attention(qs, ks, vs, us, docs, mult):
    nb = len(qs)
    keys, vals = jnp.concatenate(ks, 0), jnp.concatenate(vs, 0)
    doc_all = jnp.concatenate(docs, 0)
    outs, dqs, dk, dv, term = [], [], None, None, jnp.zeros((1, 1), F32)
    for b in range(nb):
        raw = mm_nt(qs[b], keys)
        allowed = mm_nt(docs[b], doc_all) > 0.5
        scores = jnp.where(allowed, raw * mult, -1e30)
        expo = jnp.exp(scores - jnp.max(scores, axis=1, keepdims=True))
        probs = expo * (1.0 / jnp.sum(expo, axis=1, keepdims=True))
        low = probs.astype(BF)
        att = mm(low, vals)
        delta = jnp.sum(us[b].astype(F32) * att, axis=1, keepdims=True)
        ds = probs * (mm_nt(us[b], vals) - delta)
        term += jnp.sum(jnp.sum(ds * raw, axis=1, keepdims=True), axis=0, keepdims=True)
        ds_low = ds.astype(BF)
        outs.append(att.astype(BF))
        dqs.append((mm(ds_low, keys) * mult).astype(BF))
        dk_b, dv_b = mm_tn(ds_low, qs[b]), mm_tn(low, us[b])
        dk, dv = (dk_b, dv_b) if dk is None else (dk + dk_b, dv + dv_b)
    dk = (dk * mult).astype(BF)
    dv = dv.astype(BF)
    part = lambda z: [z[b * 128 : (b + 1) * 128] for b in range(nb)]
    return outs, dqs, part(dk), part(dv), term * (1.0 / math.sqrt(D))


def doc_bounds(sizes):
    lane = iota((1, 128), 1)
    first, end = jnp.zeros((1, 128), jnp.int32), jnp.zeros((1, 128), jnp.int32)
    at = jnp.int32(0)
    for c in range(8):
        nxt = at + sizes[c] if c < 7 else jnp.int32(1 << 30)
        first, end = jnp.where(lane == c, at, first), jnp.where(lane == c, nxt, end)
        at = nxt
    return first, end


def doc_onehot(pos, bounds):
    return onehot((pos >= bounds[0]) & (pos < bounds[1]))


def at_lane(term, head):
    return jnp.where(iota((1, 128), 1) == head, term, 0.0)


def local_kernel(ids, sharp, sizes, q_ref, k_ref, v_ref, u_ref, z0_ref, terms_ref):
    here = doc_onehot(ids[0] * 128 + iota((128, 128), 0), doc_bounds(sizes))
    total = jnp.zeros((1, 128), F32)
    for h in range(2):
        blocks = [[ref[:, h * D : (h + 1) * D]] for ref in (q_ref, k_ref, v_ref, u_ref)]
        *res, term = attention(*blocks, [here], sharp[h] * (1.0 / math.sqrt(D)))
        for t in range(4):
            z0_ref[t * 128 : (t + 1) * 128, h * D : (h + 1) * D] = res[t][0]
        total += at_lane(term, h)
    terms_ref[...] = jnp.broadcast_to(total, (8, 128))


def near_kernel(ids, sharp, sizes, q_ref, k_ref, v_ref, u_ref, g1_ref, before_ref, own_ref, back_ref, terms_ref):
    dev = ids[0]
    _, _, _, r = xyqr(dev)
    row = iota((128, 128), 0)
    bounds = doc_bounds(sizes)
    here = doc_onehot(dev * 128 + row, bounds)
    there = doc_onehot((dev ^ 1) * 128 + row, bounds)
    refs = (q_ref, k_ref, v_ref, u_ref)
    h = 2 + (r & 1)
    blocks = [[cols(ref, h), g1_ref[t * 128 : (t + 1) * 128]] for t, ref in enumerate(refs)]
    *res, term = attention(*blocks, [here, there], sharp[h] * (1.0 / math.sqrt(D)))
    for t in range(4):
        own_ref[t * 128 : (t + 1) * 128] = res[t][0]
        back_ref[t * 128 : (t + 1) * 128] = res[t][1]
    terms_ref[...] = before_ref[...] + jnp.broadcast_to(at_lane(term, h), (8, 128))


def pieces(v):
    hi = v.astype(BF).astype(F32)
    mid = (v - hi).astype(BF).astype(F32)
    lo = v - hi - mid
    row = iota((16, 128), 0)
    return jnp.where(row == 0, hi, jnp.where(row == 1, mid, jnp.where(row == 2, lo, 0.0))).astype(BF)


def task_kernel(ids, sharp, sizes, i0, i1, i2, i3, terms_ref, o0, o1, o2, o3):
    ins, outs = (i0, i1, i2, i3), (o0, o1, o2, o3)
    x, y, q, r = xyqr(ids[0])
    m = iota((128, 128), 0)
    near, r3 = r < 2, r == 2
    far = r == 3
    q3 = q == 3
    u_m = jnp.where(near, q, jnp.where(r3, q ^ (m >> 6), m >> 5))
    y_m = jnp.where(far & (q == 2), y ^ ((m >> 4) & 1), jnp.where(far & q3, jnp.where(y < 2, (m >> 3) & 3, (m >> 2) & 3), y))
    x_m = jnp.where(far & q3 & (y >= 2), (m >> 4) & 1, x)
    level = jnp.where(near, 2, jnp.where(r3, 3, jnp.where(q < 2, 4, jnp.where(q == 2, 5, jnp.where(y < 2, 6, 7)))))
    j = jnp.where(near, r, jnp.where(r3, q & 1, jnp.where(q < 2, q, jnp.where(q == 2, y & 1, jnp.where(y < 2, y, x)))))
    sh = level - 2
    dil = jnp.left_shift(1, sh)
    offset = (5 + j * (dil >> 1)) & (dil - 1)
    i_m = m & (jnp.right_shift(128, sh) - 1)
    low = (x_m * 64 + y_m * 16 + u_m * 4) * 128 + i_m * dil + offset
    bounds = doc_bounds(sizes)
    docs = [doc_onehot(low + (r ^ v) * 128, bounds) for v in range(4)]
    head = level * 2 + j
    blocks = [[ref[t * 128 : (t + 1) * 128] for ref in ins] for t in range(4)]
    *res, term = attention(*blocks, docs, sharp[head] * (1.0 / math.sqrt(D)))
    extra = pieces(terms_ref[0:1] + at_lane(term, head))
    for v, ref in enumerate(outs):
        for t in range(4):
            ref[t * 128 : (t + 1) * 128] = res[t][v]
        ref[512:528] = extra


def total4(blocks):
    a, b, c, d = [jnp.sum(z.astype(F32), axis=0, keepdims=True) for z in blocks]
    return (a + b) + (c + d)


def from_r_kernel(ids, i0, i1, i2, i3, g3_ref, out_ref):
    _, _, _, r = xyqr(ids[0])
    ins = (i0, i1, i2, i3)
    for v, ref in enumerate(ins):

        @pl.when((r ^ v) == 2)
        def _():
            for t in range(4):
                g3_ref[t * 64 : (t + 1) * 64] = ref[t * 128 + 64 : t * 128 + 128]

        @pl.when((r ^ v) == 3)
        def _():
            for t in range(4):
                for u in range(4):
                    out_ref[u, t * 32 : (t + 1) * 32] = ref[t * 128 + u * 32 : t * 128 + u * 32 + 32]

    extra = pieces(total4([ref[512:528] for ref in ins]))
    for u in range(4):
        out_ref[u, 128:144] = extra


def from_q_kernel(ids, in_ref, g5_ref, out_ref):
    x, y, _, _ = xyqr(ids[0])
    dp = ids[1]
    want = xy_col(x, y, iota((256, 128), 1))
    perm = onehot(want == iota((256, 128), 0))
    extra = pieces(total4([in_ref[u, 128:144] for u in range(4)]))
    for d in range(32):
        out_ref[d, 0:32] = jnp.zeros((32, D), BF)
        out_ref[d, 32:48] = extra
    for t in range(4):
        g5_ref[t * 16 : (t + 1) * 16] = in_ref[2, t * 32 + 16 : t * 32 + 32]
    rows = mm(perm, in_ref[3, 0:128]).astype(BF)
    for d in range(8):
        out_ref[d * 4 + dp, 0:32] = rows[d * 32 : (d + 1) * 32]


def spread(level, j):
    n = 128 // DIL[level]
    return onehot(iota((128, n), 0) == iota((128, n), 1) * DIL[level] + off(level, j))


def put(ref, head, value):
    ref[:, pl.ds(pl.multiple_of(head * D, D), D)] = value.astype(BF)


def unpack_low_kernel(ids, z0_ref, own_ref, g1_ref, r0, r1, r2, r3, o_ref, dq_ref, dk_ref, dv_ref, mine_ref):
    _, _, q, r = xyqr(ids[0])
    res = (o_ref, dq_ref, dk_ref, dv_ref)
    j1, j3 = r & 1, q & 1
    for t, ref in enumerate(res):
        lo = t * 128
        ref[:, : 2 * D] = z0_ref[lo : lo + 128]
        put(ref, 2 + j1, own_ref[lo : lo + 128])
        put(ref, 3 - j1, g1_ref[lo : lo + 128])
    for v, src in enumerate((r0, r1, r2, r3)):
        role = r ^ v

        @pl.when(role < 2)
        def _():
            for t, ref in enumerate(res):
                put(ref, 4 + role, src[t * 128 : (t + 1) * 128])

        @pl.when(role == 2)
        def _():
            w3 = spread(3, j3)
            for t in range(4):
                mine_ref[t] = mm(w3, src[t * 128 : t * 128 + 64]).astype(BF)


def unpack_high_kernel(ids, l0, l1, l2, l3, mine_ref, g3_ref, qr_ref, g5_ref, xy_ref, o_ref, dq_ref, dk_ref, dv_ref, terms_ref):
    x, y, q, _ = xyqr(ids[0])
    dp = ids[1]
    res = (o_ref, dq_ref, dk_ref, dv_ref)
    j3, j5 = q & 1, y & 1
    w3b = spread(3, 1 - j3)
    w40, w41, w5, w5b = spread(4, 0), spread(4, 1), spread(5, j5), spread(5, 1 - j5)
    pi, ci = iota((128, 32), 0), iota((128, 32), 1)
    for t, ref in enumerate(res):
        put(ref, j3, mine_ref[t])
        put(ref, 1 - j3, mm(w3b, g3_ref[t * 64 : (t + 1) * 64]))
        put(ref, 2, mm(w40, qr_ref[0, t * 32 : (t + 1) * 32]))
        put(ref, 3, mm(w41, qr_ref[1, t * 32 : (t + 1) * 32]))
        put(ref, 4 + j5, mm(w5, qr_ref[2, t * 32 : t * 32 + 16]))
        put(ref, 5 - j5, mm(w5b, g5_ref[t * 16 : (t + 1) * 16]))
        for j in range(2):
            w6 = onehot(pi == (ci - t * 8) * 16 + off(6, j))
            w7 = onehot(pi == (ci - t * 4) * 32 + off(7, j))
            put(ref, 6 + j, mm(w6, xy_ref[(x * 4 + j) * 4 + dp, 0:32]))
            put(ref, 8 + j, mm(w7, xy_ref[(j * 4 + 2) * 4 + dp, 0:32]))
    acc = xy_ref[0, 32:48].astype(F32)
    for d in range(1, 32):
        acc += xy_ref[d, 32:48].astype(F32)
    terms_ref[...] = jnp.sum(acc, axis=0, keepdims=True)[:, :16]


SMEM = pl.BlockSpec(memory_space=pltpu.SMEM)
VMEM = pl.BlockSpec(memory_space=pltpu.VMEM)
LIMIT = pltpu.CompilerParams(vmem_limit_bytes=12 << 20)


def stay(array):
    return pltpu.with_memory_space_constraint(array, pltpu.VMEM)


def call(kernel, outs, scalars, params, rest, scratch=(), out_space=pltpu.VMEM):
    shapes = [out_space(s, d) for s, d in outs]
    single = len(shapes) == 1
    run = pl.pallas_call(
        kernel,
        in_specs=[SMEM] * len(scalars) + [VMEM] * (len(params) + len(rest)),
        out_specs=VMEM if single else [VMEM] * len(shapes),
        out_shape=shapes[0] if single else shapes,
        scratch_shapes=list(scratch),
        compiler_params=LIMIT,
    )
    args = [*params, *[stay(a) for a in rest]]
    return run(*scalars, *args)


def swap(array, axis, v):
    return lax.ppermute(array, axis, [(i, i ^ v) for i in range(4)])


def body(asking_vectors, lookup_vectors, payload_vectors, incoming_sensitivity, learned_sharpness, reply_list_sizes):
    raw = [a[0] for a in (asking_vectors, lookup_vectors, payload_vectors, incoming_sensitivity)]
    ids = jnp.stack([lax.axis_index(SEQ), lax.axis_index("dp")]).astype(jnp.int32)
    block = lambda n: ((n, D), BF)
    held = [pltpu.with_memory_space_constraint(a, pltpu.HBM) for a in raw]
    xy = pl.pallas_call(
        pack_kernel,
        grid=(1,),
        in_specs=[SMEM] + [pl.BlockSpec((128, 8 * D), lambda i: (0, 1))] * 4,
        out_specs=pl.BlockSpec((8, 96, D), lambda i: (0, 0, 0)),
        out_shape=jax.ShapeDtypeStruct((8, 96, D), BF),
        compiler_params=LIMIT,
        name="pack",
    )(ids, *held)
    xy = lax.all_to_all(xy, ("x", "y"), 0, 0)
    four = [stay(a) for a in raw]
    sizes = reply_list_sizes[0]
    z0, terms = call(local_kernel, [((512, 2 * D), BF), ((8, 128), F32)], [ids, learned_sharpness, sizes], four, [])
    g1, g3 = call(early_kernel, [block(512), block(256)], [ids], four, [])
    qs = call(to_q_kernel, [((4, 128, D), BF)], [ids], four, [xy])
    qs = lax.all_to_all(qs, "q", 0, 0)
    g3 = swap(g3, "q", 1)
    g1 = swap(g1, "r", 1)
    r0, r1, r2, r3 = call(to_r_kernel, [block(512)] * 4, [ids], four, [g3, qs], [pltpu.VMEM((4, 512, D), BF)])
    r1, r3, r2 = swap(r1, "r", 1), swap(r3, "r", 3), swap(r2, "r", 2)
    own1, back1, terms = call(
        near_kernel, [block(512), block(512), ((8, 128), F32)], [ids, learned_sharpness, sizes], four, [g1, terms]
    )
    back1 = swap(back1, "r", 1)
    r0, r1, r2, r3 = call(
        task_kernel, [block(528)] * 4, [ids, learned_sharpness, sizes], [],
        [r0, r1, r2, r3, terms],
    )
    r3, r2, r1 = swap(r3, "r", 3), swap(r2, "r", 2), swap(r1, "r", 1)
    back3, qs = call(from_r_kernel, [block(256), ((4, 144, D), BF)], [ids], [], [r0, r1, r2, r3])
    qs = lax.all_to_all(qs, "q", 0, 0)
    back3 = swap(back3, "q", 1)
    back5, xy = call(from_q_kernel, [block(64), ((32, 48, D), BF)], [ids], [], [qs])
    xy = lax.all_to_all(xy, ("x", "y", "dp"), 0, 0)
    back5 = swap(back5, "y", 1)
    result = jax.ShapeDtypeStruct((128, 16 * D), BF)
    args = [stay(a) for a in (z0, own1, back1, r0, r1, r2, r3)]
    *outs, mine = pl.pallas_call(
        unpack_low_kernel,
        grid=(1,),
        in_specs=[SMEM] + [VMEM] * len(args),
        out_specs=[pl.BlockSpec((128, 6 * D), lambda i: (0, 0))] * 4 + [pl.BlockSpec((4, 128, D), lambda i: (0, 0, 0))],
        out_shape=[result] * 4 + [jax.ShapeDtypeStruct((4, 128, D), BF)],
        compiler_params=LIMIT,
        name="unpack_low",
    )(ids, *args)
    args = [stay(a) for a in (mine, back3, qs, back5, xy)]
    high = pl.BlockSpec((pl.Element(128), pl.Element(10 * D)), lambda i: (0, 6 * D))
    *outs, terms = pl.pallas_call(
        unpack_high_kernel,
        grid=(1,),
        in_specs=[SMEM] + [pl.BlockSpec(memory_space=pl.ANY)] * 4 + [VMEM] * len(args),
        out_specs=[high] * 4 + [pl.BlockSpec((1, 16), lambda i: (0, 0))],
        out_shape=[result] * 4 + [jax.ShapeDtypeStruct((1, 16), F32)],
        input_output_aliases={1: 0, 2: 1, 3: 2, 4: 3},
        compiler_params=LIMIT,
        name="unpack_high",
    )(ids, *outs, *args)
    return (*[o[None] for o in outs], terms[0])


def solution(mesh):
    fine = Mesh(mesh.devices.reshape(2, 4, 4, 4, 4), SEQ + ("dp",))
    rows = P("dp", SEQ, None)
    in_specs = (rows, rows, rows, rows, P(), P("dp", None))
    out_specs = (rows, rows, rows, rows, P())
    return jax.shard_map(body, mesh=fine, in_specs=in_specs, out_specs=out_specs, check_vma=False)
```

```python
import math

import jax
import jax.numpy as jnp
from jax import lax
from jax.experimental import pallas as pl
from jax.experimental.pallas import tpu as pltpu
from jax.sharding import Mesh, PartitionSpec as P


D = 128
BF = jnp.bfloat16
F32 = jnp.float32
DIL = (1, 1, 1, 2, 4, 8, 16, 32)
SEQ = ("x", "y", "q", "r")


def off(level, j):
    dil = DIL[level]
    return (5 + j * (dil // 2)) % dil


def iota(shape, dim):
    return lax.broadcasted_iota(jnp.int32, shape, dim)


def onehot(cond):
    return cond.astype(F32).astype(BF)


def mm(a, b):
    return jnp.dot(a, b, preferred_element_type=F32)


def mm_nt(a, b):
    return lax.dot_general(a, b, (((1,), (1,)), ((), ())), preferred_element_type=F32)


def mm_tn(a, b):
    return lax.dot_general(a, b, (((0,), (0,)), ((), ())), preferred_element_type=F32)


def pick(level, j):
    n = 128 // DIL[level]
    return onehot(iota((n, 128), 1) == iota((n, 128), 0) * DIL[level] + off(level, j))


def cols(ref, head, first=0):
    return ref[:, pl.ds(pl.multiple_of((head - first) * D, D), D)]


def xyqr(dev):
    return dev >> 6, (dev >> 4) & 3, (dev >> 2) & 3, dev & 3


def xy_col(x, y, row):
    t, m = row >> 5, row & 31
    six = (x * 4 + (m >> 3)) * 32 + t * 8 + (m & 7)
    seven = (m >> 2) * 32 + t * 4 + (m & 3)
    return jnp.where(y < 2, six, jnp.where(y == 2, seven, -1))


def pack_kernel(ids, q6_ref, k6_ref, v6_ref, u6_ref, q_ref, k_ref, v_ref, u_ref, g3_ref, xy_ref):
    x, y, q, _ = xyqr(ids[0])
    srcs = (q_ref, k_ref, v_ref, u_ref)
    j5 = 1 - (y & 1)
    s5 = pick(5, j5)
    j3 = 1 - (q & 1)
    s3 = pick(3, j3)
    for t, ref in enumerate((q6_ref, k6_ref, v6_ref, u6_ref)):
        g3_ref[t * 64 : (t + 1) * 64] = mm(s3, cols(ref, j3)).astype(BF)
    xy_ref[...] = jnp.zeros(xy_ref.shape, BF)
    for t, ref in enumerate(srcs):
        xy_ref[x * 4 + (y ^ 1), 32 + t * 16 : 48 + t * 16] = mm(s5, cols(ref, 2 + j5)).astype(BF)
    for j in range(2):
        acc6 = jnp.zeros((32, D), F32)
        acc7 = jnp.zeros((32, D), F32)
        ri, ci = iota((32, 128), 0), iota((32, 128), 1)
        for t, ref in enumerate(srcs):
            w6 = onehot((ci == (ri - t * 8) * 16 + off(6, j)))
            w7 = onehot((ci == (ri - t * 4) * 32 + off(7, j)))
            acc6 += mm(w6, ref[:, (4 + j) * D : (5 + j) * D])
            acc7 += mm(w7, ref[:, (6 + j) * D : (7 + j) * D])
        xy_ref[x * 4 + j, 0:32] = acc6.astype(BF)
        xy_ref[j * 4 + 2, 0:32] = acc7.astype(BF)


def to_q_kernel(ids, q_ref, k_ref, v_ref, u_ref, xy_ref, out_ref):
    x, y, _, _ = xyqr(ids[0])
    j5 = y & 1
    s40, s41, s5 = pick(4, 0), pick(4, 1), pick(5, j5)
    for t, ref in enumerate((q_ref, k_ref, v_ref, u_ref)):
        out_ref[0, t * 32 : (t + 1) * 32] = mm(s40, ref[:, 8 * D : 9 * D]).astype(BF)
        out_ref[1, t * 32 : (t + 1) * 32] = mm(s41, ref[:, 9 * D : 10 * D]).astype(BF)
        out_ref[2, t * 32 : t * 32 + 16] = mm(s5, cols(ref, 10 + j5)).astype(BF)
        out_ref[2, t * 32 + 16 : t * 32 + 32] = xy_ref[x * 4 + (y ^ 1), 32 + t * 16 : 48 + t * 16]
    want = xy_col(x, y, iota((128, 256), 0))
    perm = onehot(want == iota((128, 256), 1))
    out_ref[3] = mm(perm, xy_ref[:, 0:32].reshape(256, D)).astype(BF)


def early_kernel(ids, q_ref, k_ref, v_ref, u_ref, g1_ref):
    h1 = 3 - (ids[0] & 1)
    for t, ref in enumerate((q_ref, k_ref, v_ref, u_ref)):
        g1_ref[t * 128 : (t + 1) * 128] = cols(ref, h1)


def to_r_kernel(ids, q_ref, k_ref, v_ref, u_ref, g3_ref, qr_ref, own_ref, t1_ref, t2_ref, t3_ref, tmp):
    _, _, q, r = xyqr(ids[0])
    j3 = q & 1
    s3 = pick(3, j3)
    for t, ref in enumerate((q_ref, k_ref, v_ref, u_ref)):
        lo = t * 128
        tmp[0, lo : lo + 128] = ref[:, 4 * D : 5 * D]
        tmp[1, lo : lo + 128] = ref[:, 5 * D : 6 * D]
        tmp[2, lo : lo + 64] = mm(s3, cols(ref, 6 + j3)).astype(BF)
        tmp[2, lo + 64 : lo + 128] = g3_ref[t * 64 : (t + 1) * 64]
        for u in range(4):
            tmp[3, lo + u * 32 : lo + u * 32 + 32] = qr_ref[u, t * 32 : (t + 1) * 32]
    for v, ref in enumerate((own_ref, t1_ref, t2_ref, t3_ref)):
        ref[...] = tmp[r ^ v]


def attention(qs, ks, vs, us, docs, mult):
    nb = len(qs)
    keys, vals = jnp.concatenate(ks, 0), jnp.concatenate(vs, 0)
    doc_all = jnp.concatenate(docs, 0)
    outs, dqs, dk, dv, term = [], [], None, None, jnp.zeros((1, 1), F32)
    for b in range(nb):
        raw = mm_nt(qs[b], keys)
        allowed = mm_nt(docs[b], doc_all) > 0.5
        scores = jnp.where(allowed, raw * mult, -1e30)
        expo = jnp.exp(scores - jnp.max(scores, axis=1, keepdims=True))
        probs = expo * (1.0 / jnp.sum(expo, axis=1, keepdims=True))
        low = probs.astype(BF)
        att = mm(low, vals)
        delta = jnp.sum(us[b].astype(F32) * att, axis=1, keepdims=True)
        ds = probs * (mm_nt(us[b], vals) - delta)
        term += jnp.sum(jnp.sum(ds * raw, axis=1, keepdims=True), axis=0, keepdims=True)
        ds_low = ds.astype(BF)
        outs.append(att.astype(BF))
        dqs.append((mm(ds_low, keys) * mult).astype(BF))
        dk_b, dv_b = mm_tn(ds_low, qs[b]), mm_tn(low, us[b])
        dk, dv = (dk_b, dv_b) if dk is None else (dk + dk_b, dv + dv_b)
    dk = (dk * mult).astype(BF)
    dv = dv.astype(BF)
    part = lambda z: [z[b * 128 : (b + 1) * 128] for b in range(nb)]
    return outs, dqs, part(dk), part(dv), term * (1.0 / math.sqrt(D))


def doc_bounds(sizes):
    lane = iota((1, 128), 1)
    first, end = jnp.zeros((1, 128), jnp.int32), jnp.zeros((1, 128), jnp.int32)
    at = jnp.int32(0)
    for c in range(8):
        nxt = at + sizes[c] if c < 7 else jnp.int32(1 << 30)
        first, end = jnp.where(lane == c, at, first), jnp.where(lane == c, nxt, end)
        at = nxt
    return first, end


def doc_onehot(pos, bounds):
    return onehot((pos >= bounds[0]) & (pos < bounds[1]))


def at_lane(term, head):
    return jnp.where(iota((1, 128), 1) == head, term, 0.0)


def local_kernel(ids, sharp, sizes, q_ref, k_ref, v_ref, u_ref, z0_ref, terms_ref):
    here = doc_onehot(ids[0] * 128 + iota((128, 128), 0), doc_bounds(sizes))
    total = jnp.zeros((1, 128), F32)
    for h in range(2):
        blocks = [[ref[:, h * D : (h + 1) * D]] for ref in (q_ref, k_ref, v_ref, u_ref)]
        *res, term = attention(*blocks, [here], sharp[h] * (1.0 / math.sqrt(D)))
        for t in range(4):
            z0_ref[t * 128 : (t + 1) * 128, h * D : (h + 1) * D] = res[t][0]
        total += at_lane(term, h)
    terms_ref[...] = jnp.broadcast_to(total, (8, 128))


def near_kernel(ids, sharp, sizes, q_ref, k_ref, v_ref, u_ref, g1_ref, before_ref, own_ref, back_ref, terms_ref):
    dev = ids[0]
    _, _, _, r = xyqr(dev)
    row = iota((128, 128), 0)
    bounds = doc_bounds(sizes)
    here = doc_onehot(dev * 128 + row, bounds)
    there = doc_onehot((dev ^ 1) * 128 + row, bounds)
    refs = (q_ref, k_ref, v_ref, u_ref)
    h = 2 + (r & 1)
    blocks = [[cols(ref, h), g1_ref[t * 128 : (t + 1) * 128]] for t, ref in enumerate(refs)]
    *res, term = attention(*blocks, [here, there], sharp[h] * (1.0 / math.sqrt(D)))
    for t in range(4):
        own_ref[t * 128 : (t + 1) * 128] = res[t][0]
        back_ref[t * 128 : (t + 1) * 128] = res[t][1]
    terms_ref[...] = before_ref[...] + jnp.broadcast_to(at_lane(term, h), (8, 128))


def pieces(v):
    hi = v.astype(BF).astype(F32)
    mid = (v - hi).astype(BF).astype(F32)
    lo = v - hi - mid
    row = iota((16, 128), 0)
    return jnp.where(row == 0, hi, jnp.where(row == 1, mid, jnp.where(row == 2, lo, 0.0))).astype(BF)


def task_kernel(ids, sharp, sizes, i0, i1, i2, i3, terms_ref, o0, o1, o2, o3):
    ins, outs = (i0, i1, i2, i3), (o0, o1, o2, o3)
    x, y, q, r = xyqr(ids[0])
    m = iota((128, 128), 0)
    near, r3 = r < 2, r == 2
    far = r == 3
    q3 = q == 3
    u_m = jnp.where(near, q, jnp.where(r3, q ^ (m >> 6), m >> 5))
    y_m = jnp.where(far & (q == 2), y ^ ((m >> 4) & 1), jnp.where(far & q3, jnp.where(y < 2, (m >> 3) & 3, (m >> 2) & 3), y))
    x_m = jnp.where(far & q3 & (y >= 2), (m >> 4) & 1, x)
    level = jnp.where(near, 2, jnp.where(r3, 3, jnp.where(q < 2, 4, jnp.where(q == 2, 5, jnp.where(y < 2, 6, 7)))))
    j = jnp.where(near, r, jnp.where(r3, q & 1, jnp.where(q < 2, q, jnp.where(q == 2, y & 1, jnp.where(y < 2, y, x)))))
    sh = level - 2
    dil = jnp.left_shift(1, sh)
    offset = (5 + j * (dil >> 1)) & (dil - 1)
    i_m = m & (jnp.right_shift(128, sh) - 1)
    low = (x_m * 64 + y_m * 16 + u_m * 4) * 128 + i_m * dil + offset
    bounds = doc_bounds(sizes)
    docs = [doc_onehot(low + (r ^ v) * 128, bounds) for v in range(4)]
    head = level * 2 + j
    blocks = [[ref[t * 128 : (t + 1) * 128] for ref in ins] for t in range(4)]
    *res, term = attention(*blocks, docs, sharp[head] * (1.0 / math.sqrt(D)))
    extra = pieces(terms_ref[0:1] + at_lane(term, head))
    for v, ref in enumerate(outs):
        for t in range(4):
            ref[t * 128 : (t + 1) * 128] = res[t][v]
        ref[512:528] = extra


def total4(blocks):
    a, b, c, d = [jnp.sum(z.astype(F32), axis=0, keepdims=True) for z in blocks]
    return (a + b) + (c + d)


def from_r_kernel(ids, i0, i1, i2, i3, g3_ref, out_ref):
    _, _, _, r = xyqr(ids[0])
    ins = (i0, i1, i2, i3)
    for v, ref in enumerate(ins):

        @pl.when((r ^ v) == 2)
        def _():
            for t in range(4):
                g3_ref[t * 64 : (t + 1) * 64] = ref[t * 128 + 64 : t * 128 + 128]

        @pl.when((r ^ v) == 3)
        def _():
            for t in range(4):
                for u in range(4):
                    out_ref[u, t * 32 : (t + 1) * 32] = ref[t * 128 + u * 32 : t * 128 + u * 32 + 32]

    extra = pieces(total4([ref[512:528] for ref in ins]))
    for u in range(4):
        out_ref[u, 128:144] = extra


def from_q_kernel(ids, in_ref, g5_ref, out_ref):
    x, y, _, _ = xyqr(ids[0])
    dp = ids[1]
    want = xy_col(x, y, iota((256, 128), 1))
    perm = onehot(want == iota((256, 128), 0))
    extra = pieces(total4([in_ref[u, 128:144] for u in range(4)]))
    for d in range(32):
        out_ref[d, 0:32] = jnp.zeros((32, D), BF)
        out_ref[d, 32:48] = extra
    for t in range(4):
        g5_ref[t * 16 : (t + 1) * 16] = in_ref[2, t * 32 + 16 : t * 32 + 32]
    rows = mm(perm, in_ref[3, 0:128]).astype(BF)
    for d in range(8):
        out_ref[d * 4 + dp, 0:32] = rows[d * 32 : (d + 1) * 32]


def spread(level, j):
    n = 128 // DIL[level]
    return onehot(iota((128, n), 0) == iota((128, n), 1) * DIL[level] + off(level, j))


def put(ref, head, value):
    ref[:, pl.ds(pl.multiple_of(head * D, D), D)] = value.astype(BF)


def unpack_low_kernel(ids, z0_ref, own_ref, g1_ref, r0, r1, r2, r3, o_ref, dq_ref, dk_ref, dv_ref, mine_ref):
    _, _, q, r = xyqr(ids[0])
    res = (o_ref, dq_ref, dk_ref, dv_ref)
    j1, j3 = r & 1, q & 1
    for t, ref in enumerate(res):
        lo = t * 128
        ref[:, : 2 * D] = z0_ref[lo : lo + 128]
        put(ref, 2 + j1, own_ref[lo : lo + 128])
        put(ref, 3 - j1, g1_ref[lo : lo + 128])
    for v, src in enumerate((r0, r1, r2, r3)):
        role = r ^ v

        @pl.when(role < 2)
        def _():
            for t, ref in enumerate(res):
                put(ref, 4 + role, src[t * 128 : (t + 1) * 128])

        @pl.when(role == 2)
        def _():
            w3 = spread(3, j3)
            for t in range(4):
                mine_ref[t] = mm(w3, src[t * 128 : t * 128 + 64]).astype(BF)


def unpack_high_kernel(ids, l0, l1, l2, l3, mine_ref, g3_ref, qr_ref, g5_ref, xy_ref, o_ref, dq_ref, dk_ref, dv_ref, terms_ref):
    x, y, q, _ = xyqr(ids[0])
    dp = ids[1]
    res = (o_ref, dq_ref, dk_ref, dv_ref)
    j3, j5 = q & 1, y & 1
    w3b = spread(3, 1 - j3)
    w40, w41, w5, w5b = spread(4, 0), spread(4, 1), spread(5, j5), spread(5, 1 - j5)
    pi, ci = iota((128, 32), 0), iota((128, 32), 1)
    for t, ref in enumerate(res):
        put(ref, j3, mine_ref[t])
        put(ref, 1 - j3, mm(w3b, g3_ref[t * 64 : (t + 1) * 64]))
        put(ref, 2, mm(w40, qr_ref[0, t * 32 : (t + 1) * 32]))
        put(ref, 3, mm(w41, qr_ref[1, t * 32 : (t + 1) * 32]))
        put(ref, 4 + j5, mm(w5, qr_ref[2, t * 32 : t * 32 + 16]))
        put(ref, 5 - j5, mm(w5b, g5_ref[t * 16 : (t + 1) * 16]))
        for j in range(2):
            w6 = onehot(pi == (ci - t * 8) * 16 + off(6, j))
            w7 = onehot(pi == (ci - t * 4) * 32 + off(7, j))
            put(ref, 6 + j, mm(w6, xy_ref[(x * 4 + j) * 4 + dp, 0:32]))
            put(ref, 8 + j, mm(w7, xy_ref[(j * 4 + 2) * 4 + dp, 0:32]))
    acc = xy_ref[0, 32:48].astype(F32)
    for d in range(1, 32):
        acc += xy_ref[d, 32:48].astype(F32)
    terms_ref[...] = jnp.sum(acc, axis=0, keepdims=True)[:, :16]


SMEM = pl.BlockSpec(memory_space=pltpu.SMEM)
VMEM = pl.BlockSpec(memory_space=pltpu.VMEM)
LIMIT = pltpu.CompilerParams(vmem_limit_bytes=12 << 20)


def stay(array):
    return pltpu.with_memory_space_constraint(array, pltpu.VMEM)


def call(kernel, outs, scalars, params, rest, scratch=(), out_space=pltpu.VMEM):
    shapes = [out_space(s, d) for s, d in outs]
    single = len(shapes) == 1
    run = pl.pallas_call(
        kernel,
        in_specs=[SMEM] * len(scalars) + [VMEM] * (len(params) + len(rest)),
        out_specs=VMEM if single else [VMEM] * len(shapes),
        out_shape=shapes[0] if single else shapes,
        scratch_shapes=list(scratch),
        compiler_params=LIMIT,
    )
    args = [*params, *[stay(a) for a in rest]]
    return run(*scalars, *args)


def swap(array, axis, v):
    return lax.ppermute(array, axis, [(i, i ^ v) for i in range(4)])


def body(asking_vectors, lookup_vectors, payload_vectors, incoming_sensitivity, learned_sharpness, reply_list_sizes):
    raw = [a[0] for a in (asking_vectors, lookup_vectors, payload_vectors, incoming_sensitivity)]
    ids = jnp.stack([lax.axis_index(SEQ), lax.axis_index("dp")]).astype(jnp.int32)
    block = lambda n: ((n, D), BF)
    held = [pltpu.with_memory_space_constraint(a, pltpu.HBM) for a in raw]
    g3, xy = pl.pallas_call(
        pack_kernel,
        grid=(1,),
        in_specs=[SMEM]
        + [pl.BlockSpec((128, 2 * D), lambda i: (0, 3))] * 4
        + [pl.BlockSpec((128, 8 * D), lambda i: (0, 1))] * 4,
        out_specs=[pl.BlockSpec((256, D), lambda i: (0, 0)), pl.BlockSpec((8, 96, D), lambda i: (0, 0, 0))],
        out_shape=[jax.ShapeDtypeStruct((256, D), BF), jax.ShapeDtypeStruct((8, 96, D), BF)],
        compiler_params=LIMIT,
        name="pack",
    )(ids, *held, *held)
    g3 = swap(g3, "q", 1)
    xy = lax.all_to_all(xy, ("x", "y"), 0, 0)
    four = [stay(a) for a in raw]
    sizes = reply_list_sizes[0]
    z0, terms = call(local_kernel, [((512, 2 * D), BF), ((8, 128), F32)], [ids, learned_sharpness, sizes], four, [])
    g1 = call(early_kernel, [block(512)], [ids], four, [])
    qs = call(to_q_kernel, [((4, 128, D), BF)], [ids], four, [xy])
    qs = lax.all_to_all(qs, "q", 0, 0)
    g1 = swap(g1, "r", 1)
    r0, r1, r2, r3 = call(to_r_kernel, [block(512)] * 4, [ids], four, [g3, qs], [pltpu.VMEM((4, 512, D), BF)])
    r1, r3, r2 = swap(r1, "r", 1), swap(r3, "r", 3), swap(r2, "r", 2)
    own1, back1, terms = call(
        near_kernel, [block(512), block(512), ((8, 128), F32)], [ids, learned_sharpness, sizes], four, [g1, terms]
    )
    back1 = swap(back1, "r", 1)
    r0, r1, r2, r3 = call(
        task_kernel, [block(528)] * 4, [ids, learned_sharpness, sizes], [],
        [r0, r1, r2, r3, terms],
    )
    r3, r2, r1 = swap(r3, "r", 3), swap(r2, "r", 2), swap(r1, "r", 1)
    back3, qs = call(from_r_kernel, [block(256), ((4, 144, D), BF)], [ids], [], [r0, r1, r2, r3])
    qs = lax.all_to_all(qs, "q", 0, 0)
    back3 = swap(back3, "q", 1)
    back5, xy = call(from_q_kernel, [block(64), ((32, 48, D), BF)], [ids], [], [qs])
    xy = lax.all_to_all(xy, ("x", "y", "dp"), 0, 0)
    back5 = swap(back5, "y", 1)
    result = jax.ShapeDtypeStruct((128, 16 * D), BF)
    args = [stay(a) for a in (z0, own1, back1, r0, r1, r2, r3)]
    *outs, mine = pl.pallas_call(
        unpack_low_kernel,
        grid=(1,),
        in_specs=[SMEM] + [VMEM] * len(args),
        out_specs=[pl.BlockSpec((128, 6 * D), lambda i: (0, 0))] * 4 + [pl.BlockSpec((4, 128, D), lambda i: (0, 0, 0))],
        out_shape=[result] * 4 + [jax.ShapeDtypeStruct((4, 128, D), BF)],
        compiler_params=LIMIT,
        name="unpack_low",
    )(ids, *args)
    args = [stay(a) for a in (mine, back3, qs, back5, xy)]
    high = pl.BlockSpec((pl.Element(128), pl.Element(10 * D)), lambda i: (0, 6 * D))
    *outs, terms = pl.pallas_call(
        unpack_high_kernel,
        grid=(1,),
        in_specs=[SMEM] + [pl.BlockSpec(memory_space=pl.ANY)] * 4 + [VMEM] * len(args),
        out_specs=[high] * 4 + [pl.BlockSpec((1, 16), lambda i: (0, 0))],
        out_shape=[result] * 4 + [jax.ShapeDtypeStruct((1, 16), F32)],
        input_output_aliases={1: 0, 2: 1, 3: 2, 4: 3},
        compiler_params=LIMIT,
        name="unpack_high",
    )(ids, *outs, *args)
    return (*[o[None] for o in outs], terms[0])


def solution(mesh):
    fine = Mesh(mesh.devices.reshape(2, 4, 4, 4, 4), SEQ + ("dp",))
    rows = P("dp", SEQ, None)
    in_specs = (rows, rows, rows, rows, P(), P("dp", None))
    out_specs = (rows, rows, rows, rows, P())
    return jax.shard_map(body, mesh=fine, in_specs=in_specs, out_specs=out_specs, check_vma=False)
```
